128 devices in a mesh: grp: 8 (over x, y_hi), blk: 16 (over y_lo, z, core).
Axes of the slice: x: 4, y: 4 (y_hi: 2, y_lo: 2; y = y_hi * 2 + y_lo), z: 4, core: 2. Of those that a mesh axis runs over, the one named last changes fastest.
Arguments:
- fluid_temp: float32 [256, 512, 768], P('grp', 'blk'), may hold values from -6 to 6
- velocity: float32 [3, 256, 512, 768], P(None, 'grp', 'blk'), may hold values from -0.5 to 0.5
- solid_temp: float32 [64, 128, 768], P('grp', 'blk'), may hold values from -6 to 6
- conductivity: float32 [3, 64, 128, 768], P(None, 'grp', 'blk'), may hold values from 0.5 to 4
- face_fluid_cell: int32 [8, 32768], P('grp', 'blk'), may hold values from 0 to 786431
- face_owner: int32 [8, 32768], P('grp', 'blk'), may hold values from 0 to 15, as said below
- face_solid_cell: int32 [8, 32768], P('grp', 'blk'), may hold values from 0 to 49151
- face_conductance: float32 [8, 32768], P('grp', 'blk'), may hold values from 0.5 to 2
Outputs:
- fluid_next: float32 [256, 512, 768], P('grp', 'blk')
- solid_next: float32 [64, 128, 768], P('grp', 'blk')
The draws below stay inside these ranges and needn't reach their ends.
Inputs may be any that keep to these rules, and one draw needn't show every extreme that they name: `face_owner`: among the rows of one device each owner appears at most 512 times; in each index of grp one owner appears exactly 512 times among the rows of every device of that index.
All inputs are finite; a program needn't handle non-finite values.
Results may differ from the reference program's by a relative error of at most 0.0003.
Values sent between devices are 32-bit elements; how exact they have to be, the bound alone decides.
A program may use at most 128 MiB of HBM per device.

```python
import math
import jax
import jax.numpy as jnp

FLUID_X = 32
FLUID_Y = 32
FLUID_Z = 768
WALL_X = 8
WALL_Y = 8
WALL_Z = 768
SLOTS = 512
SWEEPS = 4
FACES_DEV = 2048
FACES = 32768
GRID_X = 256
GRID_Y = 512
BLADE_X = 64
BLADE_Y = 128
N_GRP = 8
N_BLK = 16


def draw_face_owner(key, part):
    base_key = jax.random.fold_in(key, 7)
    key_hottest, key_rotation, key_priority = jax.random.split(base_key, 3)
    hottest = jax.random.randint(key_hottest, (N_GRP, 1, 1), 0, N_BLK).astype(jnp.int32)
    rotation = jax.random.randint(key_rotation, (N_GRP, N_BLK, 1), 0, N_BLK - 1).astype(jnp.int32)
    position = jnp.arange(FACES_DEV, dtype=jnp.int32)[None, None, :]
    offset = 1 + (position - SLOTS + rotation) % (N_BLK - 1)
    owners = jnp.where(position < SLOTS, hottest, (hottest + offset) % N_BLK)
    priority = jax.random.randint(key_priority, (N_GRP, N_BLK, FACES_DEV), 0, FACES_DEV).astype(jnp.int32) * FACES_DEV + position
    ordering = jnp.argsort(priority, axis=-1)
    owners = jnp.take_along_axis(owners, ordering, axis=-1)
    return owners.reshape(N_GRP, FACES).astype(jnp.int32)


def plant(result, key, smallest, largest):
    longest = result.shape.index(max(result.shape))
    spots = []
    for shift in (0, 1):
        where = [jax.random.randint(jax.random.fold_in(key, axis), (), 0, length) for axis, length in enumerate(result.shape)]
        where[longest] = (where[longest] + shift) % result.shape[longest]
        spots.append(tuple(where))
    return result.at[spots[0]].set(smallest).at[spots[1]].set(largest)


def levels(stream_key, extent, shards, smallest, top_value):
    loudness, own = 1.0, jax.random.fold_in(stream_key, 6)
    for dim, shards_of in shards:
        draws = jnp.exp(jax.random.uniform(jax.random.fold_in(own, dim), (shards_of,), jnp.float32, smallest / len(shards), top_value / len(shards)))
        loudness = loudness * jnp.repeat(draws, extent[dim] // shards_of).reshape([-1 if axis == dim else 1 for axis in range(len(extent))])
    return loudness


def bell_draw(key, shape, width, reach, shards=(), kind=jnp.bfloat16):
    entries = jax.random.normal(key, shape, jnp.float32) * width
    if len(shards) > 0:
        entries = levels(key, shape, shards, -0.22, 0.18) * entries
    return jnp.clip(entries, min=-reach, max=reach).astype(kind)


def setup_inputs(seed: int = 0) -> dict:
    key_list = jax.random.split(jax.random.key(seed), 9)
    return {
        "fluid_temp": bell_draw(key_list[0], (GRID_X, GRID_Y, FLUID_Z), 1.0, 6.0, ((0, 8), (1, 16)), jnp.float32),
        "velocity": jnp.clip(jax.random.uniform(key_list[1], (3, GRID_X, GRID_Y, FLUID_Z), jnp.float32, -0.5, 0.5) * levels(key_list[1], (3, GRID_X, GRID_Y, FLUID_Z), ((1, 8), (2, 16)), -0.4, 0.0), -0.5, 0.5),
        "solid_temp": bell_draw(key_list[2], (BLADE_X, BLADE_Y, WALL_Z), 1.0, 6.0, ((0, 8), (1, 16)), jnp.float32),
        "conductivity": jnp.clip(jnp.exp(math.log(4.0) - 2.0794415 * jax.random.uniform(key_list[3], (3, BLADE_X, BLADE_Y, WALL_Z), jnp.float32) ** levels(key_list[3], (3, BLADE_X, BLADE_Y, WALL_Z), ((1, 8), (2, 16)), -0.2, 0.2)), 0.5, 4.0),
        "face_fluid_cell": plant(jax.random.randint(key_list[4], (N_GRP, FACES), 0, FLUID_X * FLUID_Y * FLUID_Z), jax.random.fold_in(key_list[4], 1), 0, (FLUID_X * FLUID_Y * FLUID_Z) - 1).astype(jnp.int32),
        "face_owner": draw_face_owner(jax.random.fold_in(key_list[8], 71), 0),
        "face_solid_cell": plant(jax.random.randint(key_list[6], (N_GRP, FACES), 0, WALL_X * WALL_Y * WALL_Z), jax.random.fold_in(key_list[6], 1), 0, (WALL_X * WALL_Y * WALL_Z) - 1).astype(jnp.int32),
        "face_conductance": jnp.clip(jnp.exp(math.log(2.0) - 1.3862944 * jax.random.uniform(key_list[7], (N_GRP, FACES), jnp.float32) ** levels(key_list[7], (N_GRP, FACES), ((0, 8), (1, 16)), -0.2, 0.2)), 0.5, 2.0),
    }


time_step = 0.2
diffusivity = 0.2
capacity = 0.5


def reference(fluid_temp, velocity, solid_temp, conductivity, face_fluid_cell, face_owner, face_solid_cell, face_conductance):
    groups = jnp.arange(N_GRP, dtype=jnp.int32)[:, None]
    column = jnp.arange(FACES, dtype=jnp.int32)[None, :]
    source_block = column // FACES_DEV
    cell = face_fluid_cell
    first = cell // (FLUID_Y * FLUID_Z)
    second = (cell // FLUID_Z) % FLUID_Y
    third = cell % FLUID_Z
    fluid_index = ((groups * FLUID_X + first) * GRID_Y + source_block * FLUID_Y + second) * FLUID_Z + third
    target = face_solid_cell
    wall_first = target // (WALL_Y * WALL_Z)
    wall_second = (target // WALL_Z) % WALL_Y
    wall_third = target % WALL_Z
    solid_index = ((groups * WALL_X + wall_first) * BLADE_Y + face_owner * WALL_Y + wall_second) * WALL_Z + wall_third
    fluid_index = fluid_index.reshape(-1).astype(jnp.int32)
    solid_index = solid_index.reshape(-1).astype(jnp.int32)
    face_temp = fluid_temp.reshape(-1)[fluid_index]
    wall_temp = solid_temp.reshape(-1)[solid_index]
    flux = face_conductance.reshape(-1) * (face_temp - wall_temp)
    sink = jnp.zeros((GRID_X * GRID_Y * FLUID_Z,), fluid_temp.dtype).at[fluid_index].add(flux)
    sink = sink.reshape(fluid_temp.shape)
    deposit = jnp.zeros((BLADE_X * BLADE_Y * WALL_Z,), solid_temp.dtype).at[solid_index].add(flux)
    deposit = deposit.reshape(solid_temp.shape)

    padded = jnp.pad(fluid_temp, 1)
    flow = jnp.pad(velocity, ((0, 0), (1, 1), (1, 1), (1, 1)))
    centre = padded[1:-1, 1:-1, 1:-1]
    lows = [padded[:-2, 1:-1, 1:-1], padded[1:-1, :-2, 1:-1], padded[1:-1, 1:-1, :-2]]
    highs = [padded[2:, 1:-1, 1:-1], padded[1:-1, 2:, 1:-1], padded[1:-1, 1:-1, 2:]]
    change = jnp.zeros_like(fluid_temp)
    for axis_number in range(3):
        comp = flow[axis_number]
        middle = comp[1:-1, 1:-1, 1:-1]
        before = [comp[:-2, 1:-1, 1:-1], comp[1:-1, :-2, 1:-1], comp[1:-1, 1:-1, :-2]][axis_number]
        after = [comp[2:, 1:-1, 1:-1], comp[1:-1, 2:, 1:-1], comp[1:-1, 1:-1, 2:]][axis_number]
        low_speed = 0.5 * (before + middle)
        high_speed = 0.5 * (middle + after)
        lower = lows[axis_number]
        upper = highs[axis_number]
        inflow = jnp.maximum(low_speed, 0.0) * lower + jnp.minimum(low_speed, 0.0) * centre
        outflow = jnp.maximum(high_speed, 0.0) * centre + jnp.minimum(high_speed, 0.0) * upper
        change = change + (inflow - outflow) + diffusivity * (upper + lower - 2.0 * centre)
    fluid_next = fluid_temp + time_step * change - time_step * sink

    divisor = capacity + 2.0 * (conductivity[0] + conductivity[1] + conductivity[2])
    base = capacity * solid_temp + deposit
    current = solid_temp
    for sweep in range(SWEEPS):
        beside_all = jnp.pad(current, 1)
        beside = conductivity[0] * (beside_all[2:, 1:-1, 1:-1] + beside_all[:-2, 1:-1, 1:-1])
        beside = beside + conductivity[1] * (beside_all[1:-1, 2:, 1:-1] + beside_all[1:-1, :-2, 1:-1])
        beside = beside + conductivity[2] * (beside_all[1:-1, 1:-1, 2:] + beside_all[1:-1, 1:-1, :-2])
        current = (base + beside) / divisor
    return fluid_next, current
```

```python
import jax
import jax.numpy as jnp
from jax import lax
from jax.experimental import pallas as pl
from jax.experimental.pallas import tpu as pltpu
from jax.sharding import PartitionSpec as P

F32 = jnp.float32
BF = jnp.bfloat16
I32 = jnp.int32
MESH = pl.DeviceIdType.MESH

NX, NY, NZ = 32, 32, 768
WX, WY = 8, 8
ZB = NZ // 128
SLOTS = 512
FACES = 2048
GRP, BLK = 8, 16
ROWS = WX * WY * ZB


def split3(v):
    hi = v.astype(BF).astype(F32)
    rest = v - hi
    mid = rest.astype(BF).astype(F32)
    return hi, mid, rest - mid


def dot(a, b):
    return lax.dot_general(a, b, (((1,), (0,)), ((), ())), preferred_element_type=F32)


def dot_nt(a, b):
    return lax.dot_general(a, b, (((1,), (1,)), ((), ())), preferred_element_type=F32)


def onehot(index, count):
    rows = lax.broadcasted_iota(I32, (count, index.shape[1]), 0)
    return jnp.where(rows == index, 1.0, 0.0).astype(BF)


def face(a, b, va, vb):
    s = 0.1 * (va + vb)
    return b * s + (jnp.maximum(s, 0.0) + 0.04) * (a - b)


def shift_up(v, lane):
    r = pltpu.roll(v, 1, 1)
    first = jnp.where(lane == 0, 0.0, r[:, :128])
    return jnp.concatenate([first, r[:, 128:]], axis=1)


def shift_down(v, lane, last):
    r = pltpu.roll(v, v.shape[1] - 1, 1)
    top = jnp.where(lane == 127, last, r[:, -128:])
    return jnp.concatenate([r[:, :-128], top], axis=1)


def main_kernel(
    rows_s, cell_v, owner_v, code_v, cond_v, fluid, vel, solid, kond,
    adv_out, solid_out, flux_out,
    tg, tp, vyp, vxp, vz, adv, buf, tf_s, rank_s, snd, inc, flx, ret, rmat,
    ysnd, yrcv, cur, sysnd, syrcv, kp, inv, base, table, dep, gs, gxs,
    lsem, ssem, rsem, osem, isem, fsem, bsem,
):
    g = lax.axis_index("grp")
    b = lax.axis_index("blk")
    has = {("g", 0): g > 0, ("g", 1): g < GRP - 1, ("b", 0): b > 0, ("b", 1): b < BLK - 1}

    def neighbour(axis, side):
        step = 1 if side else -1
        return (g + step, b) if axis == "g" else (g, b + step)

    loads = []

    def load(src, dst):
        c = pltpu.make_async_copy(src, dst, lsem.at[len(loads)])
        c.start()
        loads.append(c)

    for zb in range(ZB):
        load(fluid.at[:, :, pl.ds(zb * 128, 128)], tg.at[zb])
    load(fluid, tp.at[pl.ds(1, NX), pl.ds(8, NY), :])
    load(vel.at[1], vyp.at[:, pl.ds(8, NY), :])
    load(solid, cur.at[0, pl.ds(1, WX), pl.ds(8, WY), :])
    load(vel.at[0], vxp.at[pl.ds(1, NX)])
    load(vel.at[2], vz)
    load(kond, kp)

    bar = pltpu.get_barrier_semaphore()

    def greet(k, carry):
        pl.semaphore_signal(bar, inc=1, device_id=(g, lax.rem(b + k, BLK)), device_id_type=MESH)
        return carry

    lax.fori_loop(1, BLK, greet, 0)
    for side in (0, 1):
        @pl.when(has["g", side])
        def _():
            pl.semaphore_signal(bar, inc=1, device_id=neighbour("g", side), device_id_type=MESH)

    for side in (0, 1):
        @pl.when(jnp.logical_not(has["g", side]))
        def _():
            at = 0 if side == 0 else NX + 1
            tp[at, 8:40, :] = jnp.zeros((NY, NZ), F32)
            vxp[at] = jnp.zeros((NY, NZ), F32)
            wat = 0 if side == 0 else WX + 1
            for k in range(4):
                cur[k, wat, 8:16, :] = jnp.zeros((WY, NZ), F32)

        @pl.when(jnp.logical_not(has["b", side]))
        def _():
            yrcv[side] = jnp.zeros((2, NX, NZ), F32)
            for k in range(4):
                syrcv[k, side] = jnp.zeros((WX, NZ), F32)

    owner = owner_v[...]
    own16 = onehot(owner, BLK)
    upper = jnp.where(
        lax.broadcasted_iota(I32, (128, 128), 0) <= lax.broadcasted_iota(I32, (128, 128), 1), 1.0, 0.0
    ).astype(BF)
    offset = jnp.zeros((BLK, 1), F32)
    for c in range(FACES // 128):
        mine = own16[:, c * 128:(c + 1) * 128]
        running = dot(mine, upper) + offset
        offset = running[:, 127:128]
        rank_s[:, c * 128:(c + 1) * 128] = (
            jnp.sum(jnp.where(mine.astype(F32) > 0.5, running, 0.0), axis=0, keepdims=True) - 1.0
        ).astype(I32)

    def remote(src, dst, at, device):
        return pltpu.make_async_remote_copy(
            src_ref=src, dst_ref=dst, send_sem=ssem.at[at], recv_sem=rsem.at[at],
            device_id=device, device_id_type=MESH,
        )

    def message(kind, axis, k=0):
        out = []
        for slot in (0, 1):
            side = 1 - slot
            to = neighbour(axis, side)
            if kind == "t":
                c = remote(fluid.at[NX - 1 if side else 0],
                           tp.at[NX + 1 if slot else 0, pl.ds(8, NY), :], slot, to)
            elif kind == "v":
                c = remote(vel.at[0, NX - 1 if side else 0], vxp.at[NX + 1 if slot else 0], 2 + slot, to)
            elif kind == "y":
                c = remote(ysnd.at[side], yrcv.at[slot], 4 + slot, to)
            elif kind == "sx":
                c = remote(cur.at[k, WX if side else 1, pl.ds(8, WY), :],
                           cur.at[k, WX + 1 if slot else 0, pl.ds(8, WY), :], 6 + 2 * k + slot, to)
            else:
                c = remote(sysnd.at[k, side], syrcv.at[k, slot], 14 + 2 * k + slot, to)
            out.append(c)
        return out

    def send(kind, axis, k=0):
        for slot, c in enumerate(message(kind, axis, k)):
            @pl.when(has[axis, 1 - slot])
            def _():
                c.start()

    def receive(kind, axis, k=0):
        for slot, c in enumerate(message(kind, axis, k)):
            @pl.when(has[axis, slot])
            def _():
                c.wait_recv()

    def sent(kind, axis, k=0):
        for slot, c in enumerate(message(kind, axis, k)):
            @pl.when(has[axis, 1 - slot])
            def _():
                c.wait_send()

    greeted = 15 + has["g", 0].astype(I32) + has["g", 1].astype(I32)
    pl.semaphore_wait(bar, greeted)

    send("t", "g")
    send("v", "g")
    for i in (6, 7):
        loads[i].wait()

    def pack(x, carry):
        ysnd[0, 0, pl.ds(x, 1), :] = tp[x + 1, 8:9, :]
        ysnd[1, 0, pl.ds(x, 1), :] = tp[x + 1, 39:40, :]
        ysnd[0, 1, pl.ds(x, 1), :] = vyp[x, 8:9, :]
        ysnd[1, 1, pl.ds(x, 1), :] = vyp[x, 39:40, :]
        return carry

    lax.fori_loop(0, NX, pack, 0)
    send("y", "b")
    loads[8].wait()

    def solid_send(k):
        for x in range(WX):
            sysnd[k, 0, x:x + 1, :] = cur[k, x + 1, 8:9, :]
            sysnd[k, 1, x:x + 1, :] = cur[k, x + 1, 15:16, :]
        send("sx", "g", k)
        send("sy", "b", k)

    def solid_receive(k):
        receive("sx", "g", k)
        receive("sy", "b", k)
        for x in range(WX):
            cur[k, x + 1, 7:8, :] = syrcv[k, 0, x:x + 1, :]
            cur[k, x + 1, 16:17, :] = syrcv[k, 1, x:x + 1, :]

    solid_send(0)

    for i in range(ZB):
        loads[i].wait()
    flat = tg.reshape(ZB * NX * NY, 128)

    def gather(i, carry):
        at = pl.multiple_of(i * 16, 16)
        for u in range(16):
            buf[pl.ds(at + u, 1), :] = flat[pl.ds(rows_s[0, at + u], 1), :]
        return carry

    lax.fori_loop(0, FACES // 16, gather, 0)
    lane128 = lax.broadcasted_iota(I32, (128, 128), 0)
    for c in range(FACES // 128):
        cols = slice(c * 128, (c + 1) * 128)
        block = buf[cols, :].T
        lane = cell_v[:, cols] & 127
        tf_s[:, cols] = jnp.sum(jnp.where(lane128 == lane, block, 0.0), axis=0, keepdims=True)

    code = code_v[...]
    fields = jnp.concatenate(
        list(split3(tf_s[...])) + list(split3(cond_v[...]))
        + [((code >> 8) << 8).astype(F32), (code & 255).astype(F32)], axis=0)
    many = jnp.concatenate([fields] * BLK, axis=0)
    to = lax.broadcasted_iota(I32, (8 * BLK, FACES), 0) >> 3
    many = jnp.where(to == owner, many, 0.0).astype(BF)
    placed = dot_nt(many, onehot(rank_s[...], SLOTS))
    two = placed + pltpu.roll(placed, 8 * BLK - 1, 0)
    three = two + pltpu.roll(placed, 8 * BLK - 2, 0)
    which = lax.broadcasted_iota(I32, (8 * BLK, SLOTS), 0) & 7
    snd[...] = jnp.where(which == 6, two, three)

    def row_copy(k):
        to = lax.rem(b + k, BLK)
        return pltpu.make_async_remote_copy(
            src_ref=snd.at[pl.ds(pl.multiple_of(to * 8, 8), 8), :],
            dst_ref=inc.at[pl.ds(pl.multiple_of(b * 8, 8), 8), :],
            send_sem=osem.at[k], recv_sem=isem.at[k], device_id=(g, to), device_id_type=MESH)

    def flux_copy(k):
        to = lax.rem(b + BLK - k, BLK)
        return pltpu.make_async_remote_copy(
            src_ref=flx.at[to], dst_ref=ret.at[b],
            send_sem=fsem.at[k], recv_sem=bsem.at[k], device_id=(g, to), device_id_type=MESH)

    def row_send(k, carry):
        row_copy(k).start()
        return carry

    lax.fori_loop(1, BLK, row_send, 0)

    lane = lax.broadcasted_iota(I32, (8, 128), 1)
    loads[11].wait()
    for x in range(WX):
        k0, k1, k2 = kp[0, x], kp[1, x], kp[2, x]
        r = 1.0 / (0.5 + 2.0 * (k0 + k1 + k2))
        inv[x] = r
        kp[0, x] = k0 * r
        kp[1, x] = k1 * r
        kp[2, x] = k2 * r
    for zb in range(ZB):
        for x in range(WX):
            at = zb * 64 + x * 8
            dep[at:at + 8, 0:128] = cur[0, x + 1, 8:16, zb * 128:(zb + 1) * 128]
    across = dep[:, 0:128].T
    for i, part in enumerate(split3(across)):
        table[i * 128:(i + 1) * 128, :] = part.astype(BF)
    dep[...] = jnp.zeros((ROWS, 256), F32)

    def low_x(x):
        for t in range(4):
            r = 8 * t
            gxs[r:r + 8, :] = face(tp[x, 8 + r:16 + r, :], tp[x + 1, 8 + r:16 + r, :],
                                   vxp[x, r:r + 8, :], vxp[x + 1, r:r + 8, :])

    def slab(x, carry):
        for t in range(4):
            r = 8 + 8 * t
            gs[8 * t:8 * t + 8, :] = face(tp[x + 1, r - 1:r + 7, :], tp[x + 1, r:r + 8, :],
                                          vyp[x, r - 1:r + 7, :], vyp[x, r:r + 8, :])
        gs[32:33, :] = face(tp[x + 1, 39:40, :], tp[x + 1, 40:41, :], vyp[x, 39:40, :], vyp[x, 40:41, :])
        for t in range(4):
            r = 8 * t
            here = tp[x + 1, r + 8:r + 16, :]
            high = face(here, tp[x + 2, r + 8:r + 16, :], vxp[x + 1, r:r + 8, :], vxp[x + 2, r:r + 8, :])
            low = gxs[r:r + 8, :]
            gxs[r:r + 8, :] = high
            v = vz[x, r:r + 8, :]
            bottom = face(shift_up(here, lane), here, shift_up(v, lane), v)
            last = face(here[:, -128:], 0.0, v[:, -128:], 0.0)
            top = shift_down(bottom, lane, last)
            adv[x, r:r + 8, :] = (here + (low - high) + (gs[r:r + 8, :] - gs[r + 1:r + 9, :])
                                  + (bottom - top))
        return carry

    def spread(x, carry):
        tp[x + 1, 7:8, :] = yrcv[0, 0, pl.ds(x, 1), :]
        tp[x + 1, 40:41, :] = yrcv[1, 0, pl.ds(x, 1), :]
        vyp[x, 7:8, :] = yrcv[0, 1, pl.ds(x, 1), :]
        vyp[x, 40:41, :] = yrcv[1, 1, pl.ds(x, 1), :]
        return carry

    receive("y", "b")
    lax.fori_loop(0, NX, spread, 0)
    loads[9].wait()
    loads[10].wait()
    low_x(1)
    lax.fori_loop(1, 6, slab, 0)

    pl_own = pl.ds(pl.multiple_of(b * 8, 8), 8)
    inc[pl_own, :] = snd[pl_own, :]

    def work(k):
        src = lax.rem(b + BLK - k, BLK)
        at = pl.multiple_of(src * 8, 8)
        temp = inc[pl.ds(at, 8), :]
        code = temp[6:7, :].astype(I32)
        hot = onehot(code >> 7, ROWS)
        mask = lax.broadcasted_iota(I32, (128, SLOTS), 0) == (code & 127)
        found = dot(table[...], hot)
        found = found[0:128] + found[128:256] + found[256:384]
        wall = jnp.sum(jnp.where(mask, found, 0.0), axis=0, keepdims=True)
        flux = temp[3:4, :] * (temp[0:1, :] - wall)
        flx[src] = flux
        hi = flux.astype(BF).astype(F32)
        spread = jnp.concatenate([jnp.where(mask, hi, 0.0), jnp.where(mask, flux - hi, 0.0)], axis=0)
        dep[...] += dot_nt(hot, spread.astype(BF))

    work(0)

    def owned(k, carry):
        row_copy(k).wait_recv()
        work(k)
        flux_copy(k).start()
        return carry

    lax.fori_loop(1, BLK, owned, 0)

    def sweep(k, x):
        here = cur[k, x + 1, 8:16, :]
        beside = kp[0, x] * (cur[k, x + 2, 8:16, :] + cur[k, x, 8:16, :])
        beside = beside + kp[1, x] * (cur[k, x + 1, 9:17, :] + cur[k, x + 1, 7:15, :])
        beside = beside + kp[2, x] * (shift_up(here, lane) + shift_down(here, lane, 0.0))
        return base[x] + beside

    solid_receive(0)
    for x in range(WX):
        deposit = jnp.concatenate(
            [dep[zb * 64 + x * 8:zb * 64 + x * 8 + 8, 0:128] + dep[zb * 64 + x * 8:zb * 64 + x * 8 + 8, 128:256]
             for zb in range(ZB)], axis=1)
        base[x] = (0.5 * cur[0, x + 1, 8:16, :] + deposit) * inv[x]
        cur[1, x + 1, 8:16, :] = sweep(0, x)
    solid_send(1)
    lax.fori_loop(6, 15, slab, 0)
    solid_receive(1)
    for x in range(WX):
        cur[2, x + 1, 8:16, :] = sweep(1, x)
    solid_send(2)
    lax.fori_loop(15, 24, slab, 0)
    solid_receive(2)
    for x in range(WX):
        cur[3, x + 1, 8:16, :] = sweep(2, x)
    solid_send(3)
    lax.fori_loop(24, 31, slab, 0)
    receive("t", "g")
    receive("v", "g")
    slab(31, 0)
    low_x(0)
    slab(0, 0)
    out = pltpu.make_async_copy(adv, adv_out, lsem.at[12])
    out.start()

    own_at = pl.ds(b, 1)
    ret[own_at] = flx[own_at]

    def returned(k, carry):
        flux_copy(k).wait_recv()
        return carry

    lax.fori_loop(1, BLK, returned, 0)
    for j in range(BLK):
        rmat[j:j + 1, :] = ret[j]
    stacked = jnp.concatenate(list(split3(rmat[...])), axis=0).astype(BF)
    back = dot(stacked, onehot(rank_s[...], SLOTS))
    back = back[0:16] + back[16:32] + back[32:48]
    own = lax.broadcasted_iota(I32, (BLK, FACES), 0) == owner
    flux_out[...] = jnp.sum(jnp.where(own, back, 0.0), axis=0, keepdims=True)

    solid_receive(3)
    for x in range(WX):
        solid_out[x] = sweep(3, x)

    def drained(k, carry):
        row_copy(k).wait_send()
        flux_copy(k).wait_send()
        return carry

    lax.fori_loop(1, BLK, drained, 0)
    sent("t", "g")
    sent("v", "g")
    sent("y", "b")
    for k in range(4):
        sent("sx", "g", k)
        sent("sy", "b", k)
    out.wait()


def sink_kernel(flux_v, cell_v, adv, out, weights, rowcode):
    step = pl.program_id(0)
    slabs = adv.shape[0]

    @pl.when(step == 0)
    def _():
        cell = cell_v[...]
        coarse = cell >> 8
        xy = (coarse * 43691) >> 17
        zb = (cell >> 7) - 6 * xy
        rowcode[...] = (xy >> 5) * 192 + zb * 32 + (xy & 31)
        mask = lax.broadcasted_iota(I32, (128, FACES), 0) == (cell & 127)
        flux = -0.2 * flux_v[...]
        hi = flux.astype(BF).astype(F32)
        weights[0:128, :] = jnp.where(mask, hi, 0.0).astype(BF)
        weights[128:256, :] = jnp.where(mask, flux - hi, 0.0).astype(BF)

    hot = onehot(rowcode[...] - step * (slabs * 192), slabs * 192)
    total = dot_nt(hot, weights[...])
    total = total[:, 0:128] + total[:, 128:256]
    for x in range(slabs):
        for zb in range(ZB):
            at = x * 192 + zb * 32
            cols = slice(zb * 128, (zb + 1) * 128)
            out[x, :, cols] = adv[x, :, cols] + total[at:at + 32, :]


def shards(fluid, vel, solid, kond, cell, owner, target, cond):
    coarse = cell >> 8
    xy = (coarse * 43691) >> 17
    rows = ((cell >> 7) - 6 * xy) * (NX * NY) + xy
    wxy = ((target >> 8) * 43691) >> 17
    code = (((target >> 7) - 6 * wxy) * (WX * WY) + wxy) * 128 + (target & 127)
    vmem = pl.BlockSpec(memory_space=pltpu.VMEM)
    any_ = pl.BlockSpec(memory_space=pl.ANY)
    dma = pltpu.SemaphoreType.DMA
    adv, solid_next, flux = pl.pallas_call(
        main_kernel,
        out_shape=(
            jax.ShapeDtypeStruct((NX, NY, NZ), F32),
            jax.ShapeDtypeStruct((WX, WY, NZ), F32),
            jax.ShapeDtypeStruct((1, FACES), F32),
        ),
        in_specs=[pl.BlockSpec(memory_space=pltpu.SMEM)] + [vmem] * 4 + [any_] * 4,
        out_specs=(any_, vmem, vmem),
        scratch_shapes=[
            pltpu.VMEM((ZB, NX, NY, 128), F32),
            pltpu.VMEM((NX + 2, NY + 16, NZ), F32),
            pltpu.VMEM((NX, NY + 16, NZ), F32),
            pltpu.VMEM((NX + 2, NY, NZ), F32),
            pltpu.VMEM((NX, NY, NZ), F32),
            pltpu.VMEM((NX, NY, NZ), F32),
            pltpu.VMEM((FACES, 128), F32),
            pltpu.VMEM((1, FACES), F32),
            pltpu.VMEM((1, FACES), I32),
            pltpu.VMEM((8 * BLK, SLOTS), F32),
            pltpu.VMEM((8 * BLK, SLOTS), F32),
            pltpu.VMEM((BLK, 1, SLOTS), F32),
            pltpu.VMEM((BLK, 1, SLOTS), F32),
            pltpu.VMEM((BLK, SLOTS), F32),
            pltpu.VMEM((2, 2, NX, NZ), F32),
            pltpu.VMEM((2, 2, NX, NZ), F32),
            pltpu.VMEM((4, WX + 2, 24, NZ), F32),
            pltpu.VMEM((4, 2, WX, NZ), F32),
            pltpu.VMEM((4, 2, WX, NZ), F32),
            pltpu.VMEM((3, WX, WY, NZ), F32),
            pltpu.VMEM((WX, WY, NZ), F32),
            pltpu.VMEM((WX, WY, NZ), F32),
            pltpu.VMEM((3 * 128, ROWS), BF),
            pltpu.VMEM((ROWS, 256), F32),
            pltpu.VMEM((40, NZ), F32),
            pltpu.VMEM((NY, NZ), F32),
            dma((13,)), dma((22,)), dma((22,)), dma((BLK,)), dma((BLK,)), dma((BLK,)), dma((BLK,)),
        ],
        compiler_params=pltpu.CompilerParams(
            collective_id=0, has_side_effects=True, vmem_limit_bytes=60 * 1024 * 1024),
        name="exchange",
    )(rows, cell, owner, code, cond, fluid, vel, solid, kond)
    slabs = 4
    block = pl.BlockSpec((slabs, NY, NZ), lambda i: (i, 0, 0))
    row = pl.BlockSpec((1, FACES), lambda i: (0, 0))
    fluid_next = pl.pallas_call(
        sink_kernel,
        grid=(NX // slabs,),
        out_shape=jax.ShapeDtypeStruct((NX, NY, NZ), F32),
        in_specs=[row, row, block],
        out_specs=block,
        scratch_shapes=[pltpu.VMEM((256, FACES), BF), pltpu.VMEM((1, FACES), I32)],
        name="sink",
    )(flux, cell, adv)
    return fluid_next, solid_next


def solution(mesh):
    in_specs = (
        P("grp", "blk", None),
        P(None, "grp", "blk", None),
        P("grp", "blk", None),
        P(None, "grp", "blk", None),
        P("grp", "blk"),
        P("grp", "blk"),
        P("grp", "blk"),
        P("grp", "blk"),
    )
    out_specs = (P("grp", "blk", None), P("grp", "blk", None))
    return jax.shard_map(shards, mesh=mesh, in_specs=in_specs, out_specs=out_specs, check_vma=False)
```

```python
import jax
import jax.numpy as jnp
from jax import lax
from jax.experimental import pallas as pl
from jax.experimental.pallas import tpu as pltpu
from jax.sharding import PartitionSpec as P

F32 = jnp.float32
BF = jnp.bfloat16
I32 = jnp.int32
MESH = pl.DeviceIdType.MESH

NX, NY, NZ = 32, 32, 768
WX, WY = 8, 8
ZB = NZ // 128
SLOTS = 512
FACES = 2048
GRP, BLK = 8, 16
ROWS = WX * WY * ZB
PACK = 4
SINK = 4
CUTS = (10, 26, 1)


def split3(v):
    hi = v.astype(BF).astype(F32)
    rest = v - hi
    mid = rest.astype(BF).astype(F32)
    return hi, mid, rest - mid


def dot(a, b):
    return lax.dot_general(a, b, (((1,), (0,)), ((), ())), preferred_element_type=F32)


def dot_nt(a, b):
    return lax.dot_general(a, b, (((1,), (1,)), ((), ())), preferred_element_type=F32)


def onehot(index, count):
    rows = lax.broadcasted_iota(I32, (count, index.shape[1]), 0)
    return jnp.where(rows == index, 1.0, 0.0).astype(BF)


def face(a, b, va, vb):
    w = va + vb
    return b * w + (jnp.maximum(w, 0.0) + 0.4) * (a - b)


def shift_up(v, lane):
    r = pltpu.roll(v, 1, 1)
    first = jnp.where(lane == 0, 0.0, r[:, :128])
    return jnp.concatenate([first, r[:, 128:]], axis=1)


def shift_down(v, lane, last):
    r = pltpu.roll(v, v.shape[1] - 1, 1)
    top = jnp.where(lane == 127, last, r[:, -128:])
    return jnp.concatenate([r[:, :-128], top], axis=1)


def sink_weights(flux, cell, weights, rowcode):
    xy = ((cell >> 8) * 43691) >> 17
    zb = (cell >> 7) - 6 * xy
    rowcode[...] = (xy >> 5) * 192 + zb * 32 + (xy & 31)
    mask = lax.broadcasted_iota(I32, (128, FACES), 0) == (cell & 127)
    flux = -0.2 * flux
    hi = flux.astype(BF).astype(F32)
    weights[0:128, :] = jnp.where(mask, hi, 0.0).astype(BF)
    weights[128:256, :] = jnp.where(mask, flux - hi, 0.0).astype(BF)


def sink(group, weights, rowcode):
    hot = onehot(rowcode[...] - group * (SINK * 192), SINK * 192)
    total = dot_nt(hot, weights[...])
    return total[:, 0:128] + total[:, 128:256]


def main_kernel(
    cell_v, owner_v, target_v, cond_v, fluid, vel, solid, kond,
    adv_out, solid_out,
    rows_v, rows_s,
    tg, tp, vy, vx, vz, adv, buf, tf_s, rank_s, snd, inc, flx, ret, rmat,
    xrcv, ysnd, yrcv, cur, sysnd, syrcv, kp, inv, base, table, dep, gs, gxs, weights, rowcode,
    lsem, ssem, rsem, osem, isem, fsem, bsem, wsem,
):
    g = lax.axis_index("grp")
    b = lax.axis_index("blk")
    has = {("g", 0): g > 0, ("g", 1): g < GRP - 1, ("b", 0): b > 0, ("b", 1): b < BLK - 1}

    def neighbour(axis, side):
        step = 1 if side else -1
        return (g + step, b) if axis == "g" else (g, b + step)

    cell = cell_v[...]
    cell_xy = ((cell >> 8) * 43691) >> 17
    rows_v[...] = ((cell >> 7) - 6 * cell_xy) * (NX * NY) + cell_xy
    rows_copy = pltpu.make_async_copy(rows_v, rows_s, lsem.at[12])
    rows_copy.start()
    loads = []

    def load(src, dst):
        c = pltpu.make_async_copy(src, dst, lsem.at[len(loads)])
        c.start()
        loads.append(c)

    for zb in range(ZB):
        load(fluid.at[:, :, pl.ds(zb * 128, 128)], tg.at[zb])
    load(solid, cur.at[0, pl.ds(1, WX), pl.ds(8, WY), :])
    load(fluid, tp)
    load(vel.at[1], vy)
    load(vel.at[0], vx)
    load(vel.at[2], vz)
    load(kond, kp)

    bar = pltpu.get_barrier_semaphore()

    def greet(k, carry):
        pl.semaphore_signal(bar, inc=1, device_id=(g, lax.rem(b + k, BLK)), device_id_type=MESH)
        return carry

    lax.fori_loop(1, BLK, greet, 0)
    for side in (0, 1):
        @pl.when(has["g", side])
        def _():
            pl.semaphore_signal(bar, inc=1, device_id=neighbour("g", side), device_id_type=MESH)

    for side in (0, 1):
        @pl.when(jnp.logical_not(has["g", side]))
        def _():
            xrcv[side] = jnp.zeros((2, NY, NZ), F32)
            wat = 0 if side == 0 else WX + 1
            for k in range(4):
                cur[k, wat, 8:16, :] = jnp.zeros((WY, NZ), F32)

        @pl.when(jnp.logical_not(has["b", side]))
        def _():
            yrcv[side] = jnp.zeros((2, NX, NZ), F32)
            for k in range(4):
                syrcv[k, side] = jnp.zeros((WX, NZ), F32)

    owner = owner_v[...]
    own16 = onehot(owner, BLK)
    upper = jnp.where(
        lax.broadcasted_iota(I32, (128, 128), 0) <= lax.broadcasted_iota(I32, (128, 128), 1), 1.0, 0.0
    ).astype(BF)
    offset = jnp.zeros((BLK, 1), F32)
    for c in range(FACES // 128):
        mine = own16[:, c * 128:(c + 1) * 128]
        running = dot(mine, upper) + offset
        offset = running[:, 127:128]
        rank_s[:, c * 128:(c + 1) * 128] = (
            jnp.sum(jnp.where(mine.astype(F32) > 0.5, running, 0.0), axis=0, keepdims=True) - 1.0
        ).astype(I32)

    def remote(src, dst, at, device):
        return pltpu.make_async_remote_copy(
            src_ref=src, dst_ref=dst, send_sem=ssem.at[at], recv_sem=rsem.at[at],
            device_id=device, device_id_type=MESH,
        )

    def message(kind, axis, k=0):
        out = []
        for slot in (0, 1):
            side = 1 - slot
            to = neighbour(axis, side)
            if kind == "t":
                c = remote(fluid.at[NX - 1 if side else 0],
                           xrcv.at[slot, 0], slot, to)
            elif kind == "v":
                c = remote(vel.at[0, NX - 1 if side else 0], xrcv.at[slot, 1], 2 + slot, to)
            elif kind == "y":
                c = remote(ysnd.at[side], yrcv.at[slot], 4 + slot, to)
            elif kind == "sx":
                c = remote(cur.at[k, WX if side else 1, pl.ds(8, WY), :],
                           cur.at[k, WX + 1 if slot else 0, pl.ds(8, WY), :], 6 + 2 * k + slot, to)
            else:
                c = remote(sysnd.at[k, side], syrcv.at[k, slot], 14 + 2 * k + slot, to)
            out.append(c)
        return out

    def send(kind, axis, k=0):
        for slot, c in enumerate(message(kind, axis, k)):
            @pl.when(has[axis, 1 - slot])
            def _():
                c.start()

    def receive(kind, axis, k=0):
        for slot, c in enumerate(message(kind, axis, k)):
            @pl.when(has[axis, slot])
            def _():
                c.wait_recv()

    def sent(kind, axis, k=0):
        for slot, c in enumerate(message(kind, axis, k)):
            @pl.when(has[axis, 1 - slot])
            def _():
                c.wait_send()

    def solid_send(k):
        for x in range(WX):
            sysnd[k, 0, x:x + 1, :] = cur[k, x + 1, 8:9, :]
            sysnd[k, 1, x:x + 1, :] = cur[k, x + 1, 15:16, :]
        send("sx", "g", k)
        send("sy", "b", k)

    def solid_receive(k):
        receive("sx", "g", k)
        receive("sy", "b", k)
        for x in range(WX):
            cur[k, x + 1, 7:8, :] = syrcv[k, 0, x:x + 1, :]
            cur[k, x + 1, 16:17, :] = syrcv[k, 1, x:x + 1, :]

    for i in range(ZB):
        loads[i].wait()
    rows_copy.wait()
    flat = tg.reshape(ZB * NX * NY, 128)

    def gather(i, carry):
        at = pl.multiple_of(i * 16, 16)
        for u in range(16):
            buf[pl.ds(at + u, 1), :] = flat[pl.ds(rows_s[0, at + u], 1), :]
        return carry

    lax.fori_loop(0, FACES // 16, gather, 0)
    lane128 = lax.broadcasted_iota(I32, (128, 128), 0)
    for c in range(FACES // 128):
        cols = slice(c * 128, (c + 1) * 128)
        block = buf[cols, :].T
        lane = cell_v[:, cols] & 127
        tf_s[:, cols] = jnp.sum(jnp.where(lane128 == lane, block, 0.0), axis=0, keepdims=True)

    target = target_v[...]
    target_xy = ((target >> 8) * 43691) >> 17
    code = (((target >> 7) - 6 * target_xy) * (WX * WY) + target_xy) * 128 + (target & 127)
    mine = lax.broadcasted_iota(I32, (BLK, FACES), 0) == owner
    fields = list(split3(tf_s[...])) + list(split3(cond_v[...]))
    fields += [((code >> 8) << 8).astype(F32), (code & 255).astype(F32)]
    many = jnp.concatenate([jnp.where(mine, f, 0.0).astype(BF) for f in fields], axis=0)
    placed = dot_nt(many, onehot(rank_s[...], SLOTS))
    for i, (lo, hi) in enumerate(((0, 3), (3, 6), (6, 8))):
        part = placed[lo * BLK:(lo + 1) * BLK]
        for f in range(lo + 1, hi):
            part = part + placed[f * BLK:(f + 1) * BLK]
        for j in range(BLK):
            snd[j, :, i * SLOTS:(i + 1) * SLOTS] = part[j:j + 1, :]

    def row_copy(k):
        to = lax.rem(b + k, BLK)
        return pltpu.make_async_remote_copy(
            src_ref=snd.at[to], dst_ref=inc.at[b],
            send_sem=osem.at[k], recv_sem=isem.at[k], device_id=(g, to), device_id_type=MESH)

    def flux_copy(k):
        to = lax.rem(b + BLK - k, BLK)
        return pltpu.make_async_remote_copy(
            src_ref=flx.at[to], dst_ref=ret.at[b],
            send_sem=fsem.at[k], recv_sem=bsem.at[k], device_id=(g, to), device_id_type=MESH)

    def row_send(k, carry):
        row_copy(k).start()
        return carry

    greeted = 15 + has["g", 0].astype(I32) + has["g", 1].astype(I32)
    pl.semaphore_wait(bar, greeted)
    lax.fori_loop(1, BLK, row_send, 0)

    loads[6].wait()
    solid_send(0)
    for i in (7, 8):
        loads[i].wait()

    def pack(x, carry):
        ysnd[0, 0, pl.ds(x, 1), :] = tp[x, 0:1, :]
        ysnd[1, 0, pl.ds(x, 1), :] = tp[x, NY - 1:NY, :]
        ysnd[0, 1, pl.ds(x, 1), :] = vy[x, 0:1, :]
        ysnd[1, 1, pl.ds(x, 1), :] = vy[x, NY - 1:NY, :]
        return carry

    lax.fori_loop(0, NX, pack, 0)
    send("y", "b")
    send("t", "g")
    send("v", "g")

    lane = lax.broadcasted_iota(I32, (8, 128), 1)
    loads[11].wait()
    for x in range(WX):
        k0, k1, k2 = kp[0, x], kp[1, x], kp[2, x]
        r = 1.0 / (0.5 + 2.0 * (k0 + k1 + k2))
        inv[x] = r
        kp[0, x] = k0 * r
        kp[1, x] = k1 * r
        kp[2, x] = k2 * r
    for zb in range(ZB):
        for x in range(WX):
            at = zb * 64 + x * 8
            dep[at:at + 8, 0:128] = cur[0, x + 1, 8:16, zb * 128:(zb + 1) * 128]
    across = dep[:, 0:128].T
    for i, part in enumerate(split3(across)):
        table[i * 128:(i + 1) * 128, :] = part.astype(BF)
    dep[...] = jnp.zeros((ROWS, 256), F32)

    loads[9].wait()
    loads[10].wait()
    gxs[...] = jnp.zeros((NY, NZ), F32)
    sub = lax.broadcasted_iota(I32, (8, NZ), 0)

    def slab(x, carry, end=False):
        def finish(t, lower, upper):
            r = 8 * t
            here = tp[x, r:r + 8, :]
            total = gxs[r:r + 8, :] + (lower - upper)
            if not end:
                high = face(here, tp[x + 1, r:r + 8, :], vx[x, r:r + 8, :], vx[x + 1, r:r + 8, :])
                total = total - high
                gxs[r:r + 8, :] = high
            v = vz[x, r:r + 8, :]
            bottom = face(shift_up(here, lane), here, shift_up(v, lane), v)
            last = face(here[:, -128:], 0.0, v[:, -128:], 0.0)
            top = shift_down(bottom, lane, last)
            adv[x, r:r + 8, :] = here + 0.1 * (total + (bottom - top))

        zero = jnp.zeros((8, NZ), F32)
        temp0 = vel0 = low = low_up = zero
        for t in range(4):
            r = 8 * t
            here, v = tp[x, r:r + 8, :], vy[x, r:r + 8, :]
            temp1, vel1 = pltpu.roll(here, 1, 0), pltpu.roll(v, 1, 0)
            g_t = face(jnp.where(sub == 0, temp0, temp1), here, jnp.where(sub == 0, vel0, vel1), v)
            if t == 0:
                g_t = jnp.where(sub == 0, 0.0, g_t)
            g_up = pltpu.roll(g_t, 7, 0)
            if t > 0:
                finish(t - 1, low, jnp.where(sub == 7, g_up, low_up))
            temp0, vel0, low, low_up = temp1, vel1, g_t, g_up
        finish(3, low, jnp.where(sub == 7, 0.0, low_up))
        return carry

    lax.fori_loop(0, CUTS[0], slab, 0)

    own_at = pl.ds(b, 1)
    inc[own_at] = snd[own_at]

    def owned(q, carry):
        for j in range(PACK):
            @pl.when(q * PACK + j > 0)
            def _():
                row_copy(q * PACK + j).wait_recv()

        src = [lax.rem(b + BLK - q * PACK - j, BLK) for j in range(PACK)]
        field = [jnp.concatenate([inc[i][:, f * SLOTS:(f + 1) * SLOTS] for i in src], axis=1) for f in range(3)]
        code = field[2].astype(I32)
        hot = onehot(code >> 7, ROWS)
        mask = lax.broadcasted_iota(I32, (128, PACK * SLOTS), 0) == (code & 127)
        found = dot(table[...], hot)
        found = found[0:128] + found[128:256] + found[256:384]
        wall = jnp.sum(jnp.where(mask, found, 0.0), axis=0, keepdims=True)
        flux = field[1] * (field[0] - wall)
        hi = flux.astype(BF).astype(F32)
        spread = jnp.concatenate([jnp.where(mask, hi, 0.0), jnp.where(mask, flux - hi, 0.0)], axis=0)
        for j, i in enumerate(src):
            flx[i] = flux[:, j * SLOTS:(j + 1) * SLOTS]
        dep[...] += dot_nt(hot, spread.astype(BF))
        for j in range(PACK):
            @pl.when(q * PACK + j > 0)
            def _():
                flux_copy(q * PACK + j).start()

        return carry

    lax.fori_loop(0, BLK // PACK, owned, 0)

    def sweep(k, x):
        here = cur[k, x + 1, 8:16, :]
        beside = kp[0, x] * (cur[k, x + 2, 8:16, :] + cur[k, x, 8:16, :])
        beside = beside + kp[1, x] * (cur[k, x + 1, 9:17, :] + cur[k, x + 1, 7:15, :])
        beside = beside + kp[2, x] * (shift_up(here, lane) + shift_down(here, lane, 0.0))
        return base[x] + beside

    solid_receive(0)
    for x in range(WX):
        deposit = jnp.concatenate(
            [dep[zb * 64 + x * 8:zb * 64 + x * 8 + 8, 0:128] + dep[zb * 64 + x * 8:zb * 64 + x * 8 + 8, 128:256]
             for zb in range(ZB)], axis=1)
        base[x] = (0.5 * cur[0, x + 1, 8:16, :] + deposit) * inv[x]
        cur[1, x + 1, 8:16, :] = sweep(0, x)
    solid_send(1)
    lax.fori_loop(CUTS[0], CUTS[1], slab, 0)
    solid_receive(1)
    for x in range(WX):
        cur[2, x + 1, 8:16, :] = sweep(1, x)
    solid_send(2)
    lax.fori_loop(CUTS[1], NX - 1, slab, 0)
    slab(NX - 1, 0, True)

    ret[own_at] = flx[own_at]

    def returned(k, carry):
        flux_copy(k).wait_recv()
        return carry

    lax.fori_loop(1, BLK, returned, 0)
    for j in range(BLK):
        rmat[j:j + 1, :] = ret[j]
    stacked = jnp.concatenate(list(split3(rmat[...])), axis=0).astype(BF)
    back = dot(stacked, onehot(rank_s[...], SLOTS))
    back = back[0:16] + back[16:32] + back[32:48]
    flux = jnp.sum(jnp.where(mine, back, 0.0), axis=0, keepdims=True)
    sink_weights(flux, cell_v[...], weights, rowcode)

    receive("y", "b")
    gs[...] = 0.1 * face(yrcv[0, 0], ysnd[0, 0], yrcv[0, 1], ysnd[0, 1])
    gxs[...] = 0.1 * face(ysnd[1, 0], yrcv[1, 0], ysnd[1, 1], yrcv[1, 1])

    def edge(x, carry):
        adv[x, 0:1, :] += gs[pl.ds(x, 1), :]
        adv[x, NY - 1:NY, :] -= gxs[pl.ds(x, 1), :]
        return carry

    lax.fori_loop(0, NX, edge, 0)
    receive("t", "g")
    receive("v", "g")
    adv[0] += 0.1 * face(xrcv[0, 0], tp[0], xrcv[0, 1], vx[0])
    adv[NX - 1] -= 0.1 * face(tp[NX - 1], xrcv[1, 0], vx[NX - 1], xrcv[1, 1])

    def result(i):
        at = pl.ds(i * SINK, SINK)
        return pltpu.make_async_copy(adv.at[at], adv_out.at[at], wsem.at[i])

    def sink_group(i, carry):
        total = sink(i, weights, rowcode)
        for x in range(SINK):
            for zb in range(ZB):
                at = x * 192 + zb * 32
                cols = slice(zb * 128, (zb + 1) * 128)
                adv[i * SINK + x, :, cols] += total[at:at + 32, :]
        result(i).start()
        return carry

    lax.fori_loop(0, CUTS[2], sink_group, 0)
    solid_receive(2)
    for x in range(WX):
        cur[3, x + 1, 8:16, :] = sweep(2, x)
    solid_send(3)
    lax.fori_loop(CUTS[2], NX // SINK, sink_group, 0)
    solid_receive(3)
    for x in range(WX):
        solid_out[x] = sweep(3, x)

    def drained(k, carry):
        row_copy(k).wait_send()
        flux_copy(k).wait_send()
        return carry

    lax.fori_loop(1, BLK, drained, 0)
    sent("t", "g")
    sent("v", "g")
    sent("y", "b")
    for k in range(4):
        sent("sx", "g", k)
        sent("sy", "b", k)
    for i in range(NX // SINK):
        result(i).wait()


def shards(fluid, vel, solid, kond, cell, owner, target, cond):
    vmem = pl.BlockSpec(memory_space=pltpu.VMEM)
    any_ = pl.BlockSpec(memory_space=pl.ANY)
    dma = pltpu.SemaphoreType.DMA
    return pl.pallas_call(
        main_kernel,
        out_shape=(
            jax.ShapeDtypeStruct((NX, NY, NZ), F32),
            jax.ShapeDtypeStruct((WX, WY, NZ), F32),
        ),
        in_specs=[vmem] * 4 + [any_] * 4,
        out_specs=(any_, vmem),
        scratch_shapes=[
            pltpu.VMEM((1, FACES), I32),
            pltpu.SMEM((1, FACES), I32),
            pltpu.VMEM((ZB, NX, NY, 128), F32),
            pltpu.VMEM((NX, NY, NZ), F32),
            pltpu.VMEM((NX, NY, NZ), F32),
            pltpu.VMEM((NX, NY, NZ), F32),
            pltpu.VMEM((NX, NY, NZ), F32),
            pltpu.VMEM((NX, NY, NZ), F32),
            pltpu.VMEM((FACES, 128), F32),
            pltpu.VMEM((1, FACES), F32),
            pltpu.VMEM((1, FACES), I32),
            pltpu.VMEM((BLK, 1, 3 * SLOTS), F32),
            pltpu.VMEM((BLK, 1, 3 * SLOTS), F32),
            pltpu.VMEM((BLK, 1, SLOTS), F32),
            pltpu.VMEM((BLK, 1, SLOTS), F32),
            pltpu.VMEM((BLK, SLOTS), F32),
            pltpu.VMEM((2, 2, NY, NZ), F32),
            pltpu.VMEM((2, 2, NX, NZ), F32),
            pltpu.VMEM((2, 2, NX, NZ), F32),
            pltpu.VMEM((4, WX + 2, 24, NZ), F32),
            pltpu.VMEM((4, 2, WX, NZ), F32),
            pltpu.VMEM((4, 2, WX, NZ), F32),
            pltpu.VMEM((3, WX, WY, NZ), F32),
            pltpu.VMEM((WX, WY, NZ), F32),
            pltpu.VMEM((WX, WY, NZ), F32),
            pltpu.VMEM((3 * 128, ROWS), BF),
            pltpu.VMEM((ROWS, 256), F32),
            pltpu.VMEM((NX, NZ), F32),
            pltpu.VMEM((NY, NZ), F32),
            pltpu.VMEM((256, FACES), BF),
            pltpu.VMEM((1, FACES), I32),
            dma((13,)), dma((22,)), dma((22,)), dma((BLK,)), dma((BLK,)), dma((BLK,)), dma((BLK,)), dma((NX // SINK,)),
        ],
        compiler_params=pltpu.CompilerParams(
            collective_id=0, has_side_effects=True, vmem_limit_bytes=60 * 1024 * 1024),
        name="exchange",
    )(cell, owner, target, cond, fluid, vel, solid, kond)


def solution(mesh):
    in_specs = (
        P("grp", "blk", None),
        P(None, "grp", "blk", None),
        P("grp", "blk", None),
        P(None, "grp", "blk", None),
        P("grp", "blk"),
        P("grp", "blk"),
        P("grp", "blk"),
        P("grp", "blk"),
    )
    out_specs = (P("grp", "blk", None), P("grp", "blk", None))
    return jax.shard_map(shards, mesh=mesh, in_specs=in_specs, out_specs=out_specs, check_vma=False)
```

```python
import jax
import jax.numpy as jnp
from jax import lax
from jax.experimental import pallas as pl
from jax.experimental.pallas import tpu as pltpu
from jax.sharding import PartitionSpec as P

F32 = jnp.float32
BF = jnp.bfloat16
I32 = jnp.int32
MESH = pl.DeviceIdType.MESH

NX, NY, NZ = 32, 32, 768
WX, WY = 8, 8
ZB = NZ // 128
SLOTS = 512
FACES = 2048
GRP, BLK = 8, 16
ROWS = WX * WY * ZB
PACK = 4
SINK = 4
CUTS = (15, 0, 3)


def split3(v):
    hi = v.astype(BF).astype(F32)
    rest = v - hi
    mid = rest.astype(BF).astype(F32)
    return hi, mid, rest - mid


def dot(a, b):
    return lax.dot_general(a, b, (((1,), (0,)), ((), ())), preferred_element_type=F32)


def dot_nt(a, b):
    return lax.dot_general(a, b, (((1,), (1,)), ((), ())), preferred_element_type=F32)


def onehot(index, count):
    rows = lax.broadcasted_iota(I32, (count, index.shape[1]), 0)
    return jnp.where(rows == index, 1.0, 0.0).astype(BF)


def face(a, b, va, vb):
    w = va + vb
    return b * w + (jnp.maximum(w, 0.0) + 0.4) * (a - b)


def shift_up(v, lane):
    r = pltpu.roll(v, 1, 1)
    first = jnp.where(lane == 0, 0.0, r[:, :128])
    return jnp.concatenate([first, r[:, 128:]], axis=1)


def shift_down(v, lane, last):
    r = pltpu.roll(v, v.shape[1] - 1, 1)
    top = jnp.where(lane == 127, last, r[:, -128:])
    return jnp.concatenate([r[:, :-128], top], axis=1)


def sink_weights(flux, cell, weights, rowcode):
    xy = ((cell >> 8) * 43691) >> 17
    zb = (cell >> 7) - 6 * xy
    rowcode[...] = (xy >> 5) * 192 + zb * 32 + (xy & 31)
    mask = lax.broadcasted_iota(I32, (128, FACES), 0) == (cell & 127)
    flux = -0.2 * flux
    hi = flux.astype(BF).astype(F32)
    weights[0:128, :] = jnp.where(mask, hi, 0.0).astype(BF)
    weights[128:256, :] = jnp.where(mask, flux - hi, 0.0).astype(BF)


def sink(group, weights, rowcode):
    hot = onehot(rowcode[...] - group * (SINK * 192), SINK * 192)
    total = dot_nt(hot, weights[...])
    return total[:, 0:128] + total[:, 128:256]


def main_kernel(
    cell_v, owner_v, target_v, cond_v, fluid, vel, solid, kond,
    adv, solid_out,
    rows_v, rows_s,
    tg, vy, vx, vz, buf, tf_s, rank_s, snd, inc, flx, ret, rmat,
    xrcv, ysnd, yrcv, cur, sysnd, syrcv, kp, inv, base, table, dep, gs, gxs, weights, rowcode,
    lsem, ssem, rsem, osem, isem, fsem, bsem,
):
    g = lax.axis_index("grp")
    b = lax.axis_index("blk")
    has = {("g", 0): g > 0, ("g", 1): g < GRP - 1, ("b", 0): b > 0, ("b", 1): b < BLK - 1}

    def neighbour(axis, side):
        step = 1 if side else -1
        return (g + step, b) if axis == "g" else (g, b + step)

    cell = cell_v[...]
    cell_xy = ((cell >> 8) * 43691) >> 17
    rows_v[...] = ((cell >> 7) - 6 * cell_xy) * (NX * NY) + cell_xy
    rows_copy = pltpu.make_async_copy(rows_v, rows_s, lsem.at[14])
    rows_copy.start()
    loads = []

    def load(src, dst):
        c = pltpu.make_async_copy(src, dst, lsem.at[len(loads)])
        c.start()
        loads.append(c)

    load(solid, cur.at[0, pl.ds(1, WX), pl.ds(8, WY), :])
    for zb in range(ZB):
        load(fluid.at[:, :, pl.ds(zb * 128, 128)], tg.at[zb])
    load(vel.at[1], vy)
    load(vel.at[0, pl.ds(0, 9)], vx.at[pl.ds(0, 9)])
    load(vel.at[2, pl.ds(0, 8)], vz.at[pl.ds(0, 8)])
    load(vel.at[0, pl.ds(9, NX - 9)], vx.at[pl.ds(9, NX - 9)])
    load(vel.at[2, pl.ds(8, NX - 8)], vz.at[pl.ds(8, NX - 8)])
    load(kond, kp)

    def temp(x, rows):
        return jnp.concatenate([tg[zb, x, rows, :] for zb in range(ZB)], axis=1)

    bar = pltpu.get_barrier_semaphore()

    def greet(k, carry):
        pl.semaphore_signal(bar, inc=1, device_id=(g, lax.rem(b + k, BLK)), device_id_type=MESH)
        return carry

    lax.fori_loop(1, BLK, greet, 0)
    for side in (0, 1):
        @pl.when(has["g", side])
        def _():
            pl.semaphore_signal(bar, inc=1, device_id=neighbour("g", side), device_id_type=MESH)

    for side in (0, 1):
        @pl.when(jnp.logical_not(has["g", side]))
        def _():
            xrcv[side] = jnp.zeros((2, NY, NZ), F32)
            wat = 0 if side == 0 else WX + 1
            for k in range(4):
                cur[k, wat, 8:16, :] = jnp.zeros((WY, NZ), F32)

        @pl.when(jnp.logical_not(has["b", side]))
        def _():
            yrcv[side] = jnp.zeros((2, NX, NZ), F32)
            for k in range(4):
                syrcv[k, side] = jnp.zeros((WX, NZ), F32)

    owner = owner_v[...]
    own16 = onehot(owner, BLK)
    upper = jnp.where(
        lax.broadcasted_iota(I32, (128, 128), 0) <= lax.broadcasted_iota(I32, (128, 128), 1), 1.0, 0.0
    ).astype(BF)
    inside = dot(jnp.concatenate([own16[:, c * 128:(c + 1) * 128] for c in range(FACES // 128)], axis=0), upper)
    mine = lax.broadcasted_iota(I32, (BLK, FACES), 0) == owner
    offset = jnp.full((BLK, 1), -1.0, F32)
    for c in range(FACES // 128):
        cols = slice(c * 128, (c + 1) * 128)
        running = inside[c * BLK:(c + 1) * BLK]
        rank_s[:, cols] = jnp.sum(
            jnp.where(mine[:, cols], running + offset, 0.0), axis=0, keepdims=True).astype(I32)
        offset = offset + running[:, 127:128]

    def remote(src, dst, at, device):
        return pltpu.make_async_remote_copy(
            src_ref=src, dst_ref=dst, send_sem=ssem.at[at], recv_sem=rsem.at[at],
            device_id=device, device_id_type=MESH,
        )

    def message(kind, axis, k=0):
        out = []
        for slot in (0, 1):
            side = 1 - slot
            to = neighbour(axis, side)
            if kind == "t":
                c = remote(fluid.at[NX - 1 if side else 0],
                           xrcv.at[slot, 0], slot, to)
            elif kind == "v":
                c = remote(vel.at[0, NX - 1 if side else 0], xrcv.at[slot, 1], 2 + slot, to)
            elif kind == "y":
                c = remote(ysnd.at[side], yrcv.at[slot], 4 + slot, to)
            elif kind == "sx":
                c = remote(cur.at[k, WX if side else 1, pl.ds(8, WY), :],
                           cur.at[k, WX + 1 if slot else 0, pl.ds(8, WY), :], 6 + 2 * k + slot, to)
            else:
                c = remote(sysnd.at[k, side], syrcv.at[k, slot], 14 + 2 * k + slot, to)
            out.append(c)
        return out

    def send(kind, axis, k=0):
        for slot, c in enumerate(message(kind, axis, k)):
            @pl.when(has[axis, 1 - slot])
            def _():
                c.start()

    def receive(kind, axis, k=0):
        for slot, c in enumerate(message(kind, axis, k)):
            @pl.when(has[axis, slot])
            def _():
                c.wait_recv()

    def sent(kind, axis, k=0):
        for slot, c in enumerate(message(kind, axis, k)):
            @pl.when(has[axis, 1 - slot])
            def _():
                c.wait_send()

    def solid_send(k):
        for x in range(WX):
            sysnd[k, 0, x:x + 1, :] = cur[k, x + 1, 8:9, :]
            sysnd[k, 1, x:x + 1, :] = cur[k, x + 1, 15:16, :]
        send("sx", "g", k)
        send("sy", "b", k)

    def solid_receive(k):
        receive("sx", "g", k)
        receive("sy", "b", k)
        for x in range(WX):
            cur[k, x + 1, 7:8, :] = syrcv[k, 0, x:x + 1, :]
            cur[k, x + 1, 16:17, :] = syrcv[k, 1, x:x + 1, :]

    for i in range(1, 7):
        loads[i].wait()
    rows_copy.wait()
    flat = tg.reshape(ZB * NX * NY, 128)

    def gather(i, carry):
        at = pl.multiple_of(i * 64, 64)
        for u in range(64):
            buf[pl.ds(at + u, 1), :] = flat[pl.ds(rows_s[0, at + u], 1), :]
        return carry

    lax.fori_loop(0, FACES // 64, gather, 0)
    lane128 = lax.broadcasted_iota(I32, (128, 128), 0)
    for c in range(FACES // 128):
        cols = slice(c * 128, (c + 1) * 128)
        block = buf[cols, :].T
        lane = cell_v[:, cols] & 127
        tf_s[:, cols] = jnp.sum(jnp.where(lane128 == lane, block, 0.0), axis=0, keepdims=True)

    target = target_v[...]
    target_xy = ((target >> 8) * 43691) >> 17
    code = (((target >> 7) - 6 * target_xy) * (WX * WY) + target_xy) * 128 + (target & 127)
    fields = list(split3(tf_s[...])) + list(split3(cond_v[...]))
    fields += [((code >> 8) << 8).astype(F32), (code & 255).astype(F32)]
    many = jnp.concatenate([jnp.where(mine, f, 0.0).astype(BF) for f in fields], axis=0)
    placed = dot_nt(many, onehot(rank_s[...], SLOTS))
    for i, (lo, hi) in enumerate(((0, 3), (3, 6), (6, 8))):
        part = placed[lo * BLK:(lo + 1) * BLK]
        for f in range(lo + 1, hi):
            part = part + placed[f * BLK:(f + 1) * BLK]
        for j in range(BLK):
            snd[j, :, i * SLOTS:(i + 1) * SLOTS] = part[j:j + 1, :]

    def row_copy(k):
        to = lax.rem(b + k, BLK)
        return pltpu.make_async_remote_copy(
            src_ref=snd.at[to], dst_ref=inc.at[b],
            send_sem=osem.at[k], recv_sem=isem.at[k], device_id=(g, to), device_id_type=MESH)

    def flux_copy(k):
        to = lax.rem(b + BLK - k, BLK)
        return pltpu.make_async_remote_copy(
            src_ref=flx.at[to], dst_ref=ret.at[b],
            send_sem=fsem.at[k], recv_sem=bsem.at[k], device_id=(g, to), device_id_type=MESH)

    def row_send(k, carry):
        row_copy(k).start()
        return carry

    greeted = 15 + has["g", 0].astype(I32) + has["g", 1].astype(I32)
    pl.semaphore_wait(bar, greeted)
    lax.fori_loop(1, BLK, row_send, 0)

    loads[0].wait()
    solid_send(0)
    loads[7].wait()
    lane = lax.broadcasted_iota(I32, (8, 128), 1)

    def pack(x, carry):
        for side, rows in ((0, slice(0, 1)), (1, slice(NY - 1, NY))):
            ysnd[side, 0, pl.ds(x, 1), :] = temp(x, rows)
            ysnd[side, 1, pl.ds(x, 1), :] = vy[x, rows, :]
        return carry

    lax.fori_loop(0, NX, pack, 0)
    send("y", "b")
    send("t", "g")
    send("v", "g")

    loads[12].wait()
    for x in range(WX):
        k0, k1, k2 = kp[0, x], kp[1, x], kp[2, x]
        r = 1.0 / (0.5 + 2.0 * (k0 + k1 + k2))
        inv[x] = r
        kp[0, x] = k0 * r
        kp[1, x] = k1 * r
        kp[2, x] = k2 * r
    for zb in range(ZB):
        for x in range(WX):
            at = zb * 64 + x * 8
            dep[at:at + 8, 0:128] = cur[0, x + 1, 8:16, zb * 128:(zb + 1) * 128]
    across = dep[:, 0:128].T
    for i, part in enumerate(split3(across)):
        table[i * 128:(i + 1) * 128, :] = part.astype(BF)
    dep[...] = jnp.zeros((ROWS, 256), F32)

    for i in range(8, 12):
        loads[i].wait()
    gxs[...] = jnp.zeros((NY, NZ), F32)
    sub = lax.broadcasted_iota(I32, (8, NZ), 0)

    def slab(x, carry, end=False):
        def finish(t, lower, upper):
            r = 8 * t
            here = temp(x, slice(r, r + 8))
            total = gxs[r:r + 8, :] + (lower - upper)
            if not end:
                high = face(here, temp(x + 1, slice(r, r + 8)), vx[x, r:r + 8, :], vx[x + 1, r:r + 8, :])
                total = total - high
                gxs[r:r + 8, :] = high
            v = vz[x, r:r + 8, :]
            bottom = face(shift_up(here, lane), here, shift_up(v, lane), v)
            last = face(here[:, -128:], 0.0, v[:, -128:], 0.0)
            top = shift_down(bottom, lane, last)
            adv[x, r:r + 8, :] = here + 0.1 * (total + (bottom - top))

        zero = jnp.zeros((8, NZ), F32)
        temp0 = vel0 = low = low_up = zero
        for t in range(4):
            r = 8 * t
            here, v = temp(x, slice(r, r + 8)), vy[x, r:r + 8, :]
            temp1, vel1 = pltpu.roll(here, 1, 0), pltpu.roll(v, 1, 0)
            g_t = face(jnp.where(sub == 0, temp0, temp1), here, jnp.where(sub == 0, vel0, vel1), v)
            if t == 0:
                g_t = jnp.where(sub == 0, 0.0, g_t)
            g_up = pltpu.roll(g_t, 7, 0)
            if t > 0:
                finish(t - 1, low, jnp.where(sub == 7, g_up, low_up))
            temp0, vel0, low, low_up = temp1, vel1, g_t, g_up
        finish(3, low, jnp.where(sub == 7, 0.0, low_up))
        return carry

    lax.fori_loop(0, CUTS[0], slab, 0)

    own_at = pl.ds(b, 1)
    inc[own_at] = snd[own_at]

    def owned(q, carry):
        for j in range(PACK):
            @pl.when(q * PACK + j > 0)
            def _():
                row_copy(q * PACK + j).wait_recv()

        src = [lax.rem(b + BLK - q * PACK - j, BLK) for j in range(PACK)]
        field = [jnp.concatenate([inc[i][:, f * SLOTS:(f + 1) * SLOTS] for i in src], axis=1) for f in range(3)]
        code = field[2].astype(I32)
        hot = onehot(code >> 7, ROWS)
        mask = lax.broadcasted_iota(I32, (128, PACK * SLOTS), 0) == (code & 127)
        found = dot(table[...], hot)
        found = found[0:128] + found[128:256] + found[256:384]
        wall = jnp.sum(jnp.where(mask, found, 0.0), axis=0, keepdims=True)
        flux = field[1] * (field[0] - wall)
        hi = flux.astype(BF).astype(F32)
        spread = jnp.concatenate([jnp.where(mask, hi, 0.0), jnp.where(mask, flux - hi, 0.0)], axis=0)
        for j, i in enumerate(src):
            flx[i] = flux[:, j * SLOTS:(j + 1) * SLOTS]
        dep[...] += dot_nt(hot, spread.astype(BF))
        for j in range(PACK):
            @pl.when(q * PACK + j > 0)
            def _():
                flux_copy(q * PACK + j).start()

        return carry

    lax.fori_loop(0, BLK // PACK, owned, 0)

    def sweep(k, x):
        here = cur[k, x + 1, 8:16, :]
        beside = kp[0, x] * (cur[k, x + 2, 8:16, :] + cur[k, x, 8:16, :])
        beside = beside + kp[1, x] * (cur[k, x + 1, 9:17, :] + cur[k, x + 1, 7:15, :])
        beside = beside + kp[2, x] * (shift_up(here, lane) + shift_down(here, lane, 0.0))
        return base[x] + beside

    solid_receive(0)
    for x in range(WX):
        deposit = jnp.concatenate(
            [dep[zb * 64 + x * 8:zb * 64 + x * 8 + 8, 0:128] + dep[zb * 64 + x * 8:zb * 64 + x * 8 + 8, 128:256]
             for zb in range(ZB)], axis=1)
        base[x] = (0.5 * cur[0, x + 1, 8:16, :] + deposit) * inv[x]
        cur[1, x + 1, 8:16, :] = sweep(0, x)
    solid_send(1)
    lax.fori_loop(CUTS[0], NX - 1, slab, 0)
    slab(NX - 1, 0, True)
    solid_receive(1)
    for x in range(WX):
        cur[2, x + 1, 8:16, :] = sweep(1, x)
    solid_send(2)
    ret[own_at] = flx[own_at]

    def returned(k, carry):
        flux_copy(k).wait_recv()
        return carry

    lax.fori_loop(1, BLK, returned, 0)
    for j in range(BLK):
        rmat[j:j + 1, :] = ret[j]
    stacked = jnp.concatenate(list(split3(rmat[...])), axis=0).astype(BF)
    back = dot(stacked, onehot(rank_s[...], SLOTS))
    back = back[0:16] + back[16:32] + back[32:48]
    flux = jnp.sum(jnp.where(mine, back, 0.0), axis=0, keepdims=True)
    sink_weights(flux, cell_v[...], weights, rowcode)

    receive("y", "b")
    gs[...] = 0.1 * face(yrcv[0, 0], ysnd[0, 0], yrcv[0, 1], ysnd[0, 1])
    gxs[...] = 0.1 * face(ysnd[1, 0], yrcv[1, 0], ysnd[1, 1], yrcv[1, 1])

    def edge(x, carry):
        adv[x, 0:1, :] += gs[pl.ds(x, 1), :]
        adv[x, NY - 1:NY, :] -= gxs[pl.ds(x, 1), :]
        return carry

    lax.fori_loop(0, NX, edge, 0)
    receive("t", "g")
    receive("v", "g")
    adv[0] += 0.1 * face(xrcv[0, 0], temp(0, slice(0, NY)), xrcv[0, 1], vx[0])
    adv[NX - 1] -= 0.1 * face(temp(NX - 1, slice(0, NY)), xrcv[1, 0], vx[NX - 1], xrcv[1, 1])

    def sink_group(i, carry):
        total = sink(i, weights, rowcode)
        for x in range(SINK):
            for zb in range(ZB):
                at = x * 192 + zb * 32
                cols = slice(zb * 128, (zb + 1) * 128)
                adv[i * SINK + x, :, cols] += total[at:at + 32, :]
        return carry

    lax.fori_loop(0, CUTS[2], sink_group, 0)
    solid_receive(2)
    for x in range(WX):
        cur[3, x + 1, 8:16, :] = sweep(2, x)
    solid_send(3)
    lax.fori_loop(CUTS[2], NX // SINK, sink_group, 0)
    solid_receive(3)
    for x in range(WX):
        solid_out[x] = sweep(3, x)

    def drained(k, carry):
        row_copy(k).wait_send()
        flux_copy(k).wait_send()
        return carry

    lax.fori_loop(1, BLK, drained, 0)
    sent("t", "g")
    sent("v", "g")
    sent("y", "b")
    for k in range(4):
        sent("sx", "g", k)
        sent("sy", "b", k)


def shards(fluid, vel, solid, kond, cell, owner, target, cond):
    vmem = pl.BlockSpec(memory_space=pltpu.VMEM)
    hbm = pl.BlockSpec(memory_space=pltpu.HBM)
    dma = pltpu.SemaphoreType.DMA
    return pl.pallas_call(
        main_kernel,
        out_shape=(
            pltpu.VMEM((NX, NY, NZ), F32),
            pltpu.VMEM((WX, WY, NZ), F32),
        ),
        in_specs=[vmem] * 4 + [hbm] * 4,
        out_specs=(vmem, vmem),
        scratch_shapes=[
            pltpu.VMEM((1, FACES), I32),
            pltpu.SMEM((1, FACES), I32),
            pltpu.VMEM((ZB, NX, NY, 128), F32),
            pltpu.VMEM((NX, NY, NZ), F32),
            pltpu.VMEM((NX, NY, NZ), F32),
            pltpu.VMEM((NX, NY, NZ), F32),
            pltpu.VMEM((FACES, 128), F32),
            pltpu.VMEM((1, FACES), F32),
            pltpu.VMEM((1, FACES), I32),
            pltpu.VMEM((BLK, 1, 3 * SLOTS), F32),
            pltpu.VMEM((BLK, 1, 3 * SLOTS), F32),
            pltpu.VMEM((BLK, 1, SLOTS), F32),
            pltpu.VMEM((BLK, 1, SLOTS), F32),
            pltpu.VMEM((BLK, SLOTS), F32),
            pltpu.VMEM((2, 2, NY, NZ), F32),
            pltpu.VMEM((2, 2, NX, NZ), F32),
            pltpu.VMEM((2, 2, NX, NZ), F32),
            pltpu.VMEM((4, WX + 2, 24, NZ), F32),
            pltpu.VMEM((4, 2, WX, NZ), F32),
            pltpu.VMEM((4, 2, WX, NZ), F32),
            pltpu.VMEM((3, WX, WY, NZ), F32),
            pltpu.VMEM((WX, WY, NZ), F32),
            pltpu.VMEM((WX, WY, NZ), F32),
            pltpu.VMEM((3 * 128, ROWS), BF),
            pltpu.VMEM((ROWS, 256), F32),
            pltpu.VMEM((NX, NZ), F32),
            pltpu.VMEM((NY, NZ), F32),
            pltpu.VMEM((256, FACES), BF),
            pltpu.VMEM((1, FACES), I32),
            dma((15,)), dma((22,)), dma((22,)), dma((BLK,)), dma((BLK,)), dma((BLK,)), dma((BLK,)),
        ],
        compiler_params=pltpu.CompilerParams(
            collective_id=0, has_side_effects=True, vmem_limit_bytes=60 * 1024 * 1024),
        name="exchange",
    )(cell, owner, target, cond, fluid, vel, solid, kond)


def solution(mesh):
    in_specs = (
        P("grp", "blk", None),
        P(None, "grp", "blk", None),
        P("grp", "blk", None),
        P(None, "grp", "blk", None),
        P("grp", "blk"),
        P("grp", "blk"),
        P("grp", "blk"),
        P("grp", "blk"),
    )
    out_specs = (P("grp", "blk", None), P("grp", "blk", None))
    return jax.shard_map(shards, mesh=mesh, in_specs=in_specs, out_specs=out_specs, check_vma=False)
```

```python
import jax
import jax.numpy as jnp
from jax import lax
from jax.experimental import pallas as pl
from jax.experimental.pallas import tpu as pltpu
from jax.sharding import PartitionSpec as P

F32 = jnp.float32
BF = jnp.bfloat16
I32 = jnp.int32
MESH = pl.DeviceIdType.MESH

NX, NY, NZ = 32, 32, 768
WX, WY = 8, 8
ZB = NZ // 128
SLOTS = 512
FACES = 2048
GRP, BLK = 8, 16
ROWS = WX * WY * ZB
PACK = 4
SINK = 4
CUTS = (24, 0, 3)


def split3(v):
    hi = v.astype(BF).astype(F32)
    rest = v - hi
    mid = rest.astype(BF).astype(F32)
    return hi, mid, rest - mid


def dot(a, b):
    return lax.dot_general(a, b, (((1,), (0,)), ((), ())), preferred_element_type=F32)


def dot_nt(a, b):
    return lax.dot_general(a, b, (((1,), (1,)), ((), ())), preferred_element_type=F32)


def onehot(index, count):
    rows = lax.broadcasted_iota(I32, (count, index.shape[1]), 0)
    return jnp.where(rows == index, 1.0, 0.0).astype(BF)


def face(a, b, va, vb):
    w = va + vb
    return b * w + (jnp.maximum(w, 0.0) + 0.4) * (a - b)


def shift_up(v, lane):
    r = pltpu.roll(v, 1, 1)
    first = jnp.where(lane == 0, 0.0, r[:, :128])
    return jnp.concatenate([first, r[:, 128:]], axis=1)


def shift_down(v, lane, last):
    r = pltpu.roll(v, v.shape[1] - 1, 1)
    top = jnp.where(lane == 127, last, r[:, -128:])
    return jnp.concatenate([r[:, :-128], top], axis=1)


def sink_weights(flux, cell, weights, rowcode):
    xy = ((cell >> 8) * 43691) >> 17
    zb = (cell >> 7) - 6 * xy
    rowcode[...] = (xy >> 5) * 192 + zb * 32 + (xy & 31)
    mask = lax.broadcasted_iota(I32, (128, FACES), 0) == (cell & 127)
    flux = -0.2 * flux
    hi = flux.astype(BF).astype(F32)
    weights[0:128, :] = jnp.where(mask, hi, 0.0).astype(BF)
    weights[128:256, :] = jnp.where(mask, flux - hi, 0.0).astype(BF)


def sink(group, weights, rowcode):
    hot = onehot(rowcode[...] - group * (SINK * 192), SINK * 192)
    total = dot_nt(hot, weights[...])
    return total[:, 0:128] + total[:, 128:256]


def main_kernel(
    cell_v, owner_v, target_v, cond_v, fluid, vel, solid, kond,
    adv, solid_out,
    rows_v, rows_s,
    tg, vy, vx, vz, buf, tf_s, rank_s, snd, inc, flx, ret, rmat,
    xrcv, ysnd, yrcv, cur, sysnd, syrcv, kp, inv, base, table, dep, gs, gxs, weights, rowcode,
    lsem, ssem, rsem, osem, isem, fsem, bsem,
):
    g = lax.axis_index("grp")
    b = lax.axis_index("blk")
    has = {("g", 0): g > 0, ("g", 1): g < GRP - 1, ("b", 0): b > 0, ("b", 1): b < BLK - 1}

    def neighbour(axis, side):
        step = 1 if side else -1
        return (g + step, b) if axis == "g" else (g, b + step)

    cell = cell_v[...]
    cell_xy = ((cell >> 8) * 43691) >> 17
    cell_row = ((cell >> 7) - 6 * cell_xy) * (NX * NY) + cell_xy
    for c in range(FACES // 128):
        rows_v[c:c + 1, :] = cell_row[:, c * 128:(c + 1) * 128]
    rows_copy = pltpu.make_async_copy(rows_v, rows_s, lsem.at[14])
    rows_copy.start()
    loads = []

    def load(src, dst):
        c = pltpu.make_async_copy(src, dst, lsem.at[len(loads)])
        c.start()
        loads.append(c)

    load(solid, cur.at[0, pl.ds(1, WX), pl.ds(8, WY), :])
    for zb in range(ZB):
        load(fluid.at[:, :, pl.ds(zb * 128, 128)], tg.at[zb])

    def temp(x, rows):
        return jnp.concatenate([tg[zb, x, rows, :] for zb in range(ZB)], axis=1)

    bar = pltpu.get_barrier_semaphore()

    def greet(k, carry):
        pl.semaphore_signal(bar, inc=1, device_id=(g, lax.rem(b + k, BLK)), device_id_type=MESH)
        return carry

    lax.fori_loop(1, BLK, greet, 0)
    for side in (0, 1):
        @pl.when(has["g", side])
        def _():
            pl.semaphore_signal(bar, inc=1, device_id=neighbour("g", side), device_id_type=MESH)

    for side in (0, 1):
        @pl.when(jnp.logical_not(has["g", side]))
        def _():
            xrcv[side] = jnp.zeros((2, NY, NZ), F32)
            wat = 0 if side == 0 else WX + 1
            for k in range(4):
                cur[k, wat, 8:16, :] = jnp.zeros((WY, NZ), F32)

        @pl.when(jnp.logical_not(has["b", side]))
        def _():
            yrcv[side] = jnp.zeros((2, NX, NZ), F32)
            for k in range(4):
                syrcv[k, side] = jnp.zeros((WX, NZ), F32)

    owner = owner_v[...]
    own16 = onehot(owner, BLK)
    upper = jnp.where(
        lax.broadcasted_iota(I32, (128, 128), 0) <= lax.broadcasted_iota(I32, (128, 128), 1), 1.0, 0.0
    ).astype(BF)
    inside = dot(jnp.concatenate([own16[:, c * 128:(c + 1) * 128] for c in range(FACES // 128)], axis=0), upper)
    mine = lax.broadcasted_iota(I32, (BLK, FACES), 0) == owner
    offset = jnp.full((BLK, 1), -1.0, F32)
    for c in range(FACES // 128):
        cols = slice(c * 128, (c + 1) * 128)
        running = inside[c * BLK:(c + 1) * BLK]
        rank_s[:, cols] = jnp.sum(
            jnp.where(mine[:, cols], running + offset, 0.0), axis=0, keepdims=True).astype(I32)
        offset = offset + running[:, 127:128]

    def remote(src, dst, at, device):
        return pltpu.make_async_remote_copy(
            src_ref=src, dst_ref=dst, send_sem=ssem.at[at], recv_sem=rsem.at[at],
            device_id=device, device_id_type=MESH,
        )

    def message(kind, axis, k=0):
        out = []
        for slot in (0, 1):
            side = 1 - slot
            to = neighbour(axis, side)
            if kind == "t":
                c = remote(fluid.at[NX - 1 if side else 0],
                           xrcv.at[slot, 0], slot, to)
            elif kind == "v":
                c = remote(vel.at[0, NX - 1 if side else 0], xrcv.at[slot, 1], 2 + slot, to)
            elif kind == "y":
                c = remote(ysnd.at[side], yrcv.at[slot], 4 + slot, to)
            elif kind == "sx":
                c = remote(cur.at[k, WX if side else 1, pl.ds(8, WY), :],
                           cur.at[k, WX + 1 if slot else 0, pl.ds(8, WY), :], 6 + 2 * k + slot, to)
            else:
                c = remote(sysnd.at[k, side], syrcv.at[k, slot], 14 + 2 * k + slot, to)
            out.append(c)
        return out

    def send(kind, axis, k=0):
        for slot, c in enumerate(message(kind, axis, k)):
            @pl.when(has[axis, 1 - slot])
            def _():
                c.start()

    def receive(kind, axis, k=0):
        for slot, c in enumerate(message(kind, axis, k)):
            @pl.when(has[axis, slot])
            def _():
                c.wait_recv()

    def sent(kind, axis, k=0):
        for slot, c in enumerate(message(kind, axis, k)):
            @pl.when(has[axis, 1 - slot])
            def _():
                c.wait_send()

    def solid_send(k):
        for x in range(WX):
            sysnd[k, 0, x:x + 1, :] = cur[k, x + 1, 8:9, :]
            sysnd[k, 1, x:x + 1, :] = cur[k, x + 1, 15:16, :]
        send("sx", "g", k)
        send("sy", "b", k)

    def solid_receive(k):
        receive("sx", "g", k)
        receive("sy", "b", k)
        for x in range(WX):
            cur[k, x + 1, 7:8, :] = syrcv[k, 0, x:x + 1, :]
            cur[k, x + 1, 16:17, :] = syrcv[k, 1, x:x + 1, :]

    for i in range(1, 7):
        loads[i].wait()
    load(vel.at[1], vy)
    load(vel.at[0], vx)
    load(vel.at[2], vz)
    load(kond, kp)
    rows_copy.wait()
    flat = tg.reshape(ZB * NX * NY, 128)

    def gather(i, carry):
        at = pl.multiple_of(i * 128, 128)
        for u in range(128):
            buf[pl.ds(at + u, 1), :] = flat[pl.ds(rows_s[i, u], 1), :]
        return carry

    lax.fori_loop(0, FACES // 128, gather, 0)
    lane128 = lax.broadcasted_iota(I32, (128, 128), 0)
    for c in range(FACES // 128):
        cols = slice(c * 128, (c + 1) * 128)
        block = buf[cols, :].T
        lane = cell_v[:, cols] & 127
        tf_s[:, cols] = jnp.sum(jnp.where(lane128 == lane, block, 0.0), axis=0, keepdims=True)

    target = target_v[...]
    target_xy = ((target >> 8) * 43691) >> 17
    code = (((target >> 7) - 6 * target_xy) * (WX * WY) + target_xy) * 128 + (target & 127)
    fields = list(split3(tf_s[...])) + list(split3(cond_v[...]))
    fields += [((code >> 8) << 8).astype(F32), (code & 255).astype(F32)]
    many = jnp.concatenate([jnp.where(mine, f, 0.0).astype(BF) for f in fields], axis=0)
    placed = dot_nt(many, onehot(rank_s[...], SLOTS))
    for i, (lo, hi) in enumerate(((0, 3), (3, 6), (6, 8))):
        part = placed[lo * BLK:(lo + 1) * BLK]
        for f in range(lo + 1, hi):
            part = part + placed[f * BLK:(f + 1) * BLK]
        for j in range(BLK):
            snd[j, :, i * SLOTS:(i + 1) * SLOTS] = part[j:j + 1, :]

    def row_copy(to, src):
        return pltpu.make_async_remote_copy(
            src_ref=snd.at[to], dst_ref=inc.at[b],
            send_sem=osem.at[to], recv_sem=isem.at[src], device_id=(g, to), device_id_type=MESH)

    def flux_copy(to, src):
        return pltpu.make_async_remote_copy(
            src_ref=flx.at[to], dst_ref=ret.at[b],
            send_sem=fsem.at[to], recv_sem=bsem.at[src], device_id=(g, to), device_id_type=MESH)

    def row_send(k, carry):
        row_copy(lax.rem(b + k, BLK), b).start()
        return carry

    greeted = 15 + has["g", 0].astype(I32) + has["g", 1].astype(I32)
    pl.semaphore_wait(bar, greeted)
    lax.fori_loop(1, BLK, row_send, 0)

    loads[0].wait()
    solid_send(0)
    loads[7].wait()
    lane = lax.broadcasted_iota(I32, (8, 128), 1)

    def pack(x, carry):
        for side, rows in ((0, slice(0, 1)), (1, slice(NY - 1, NY))):
            ysnd[side, 0, pl.ds(x, 1), :] = temp(x, rows)
            ysnd[side, 1, pl.ds(x, 1), :] = vy[x, rows, :]
        return carry

    lax.fori_loop(0, NX, pack, 0)
    send("y", "b")
    loads[10].wait()
    for x in range(WX):
        k0, k1, k2 = kp[0, x], kp[1, x], kp[2, x]
        r = 1.0 / (0.5 + 2.0 * (k0 + k1 + k2))
        inv[x] = r
        kp[0, x] = k0 * r
        kp[1, x] = k1 * r
        kp[2, x] = k2 * r
    for zb in range(ZB):
        for x in range(WX):
            at = zb * 64 + x * 8
            dep[at:at + 8, 0:128] = cur[0, x + 1, 8:16, zb * 128:(zb + 1) * 128]
    across = dep[:, 0:128].T
    for i, part in enumerate(split3(across)):
        table[i * 128:(i + 1) * 128, :] = part.astype(BF)
    dep[...] = jnp.zeros((ROWS, 256), F32)

    for i in range(8, 10):
        loads[i].wait()
    gxs[...] = jnp.zeros((NY, NZ), F32)
    sub = lax.broadcasted_iota(I32, (8, NZ), 0)

    def slab(x, carry, end=False):
        def finish(t, lower, upper):
            r = 8 * t
            here = temp(x, slice(r, r + 8))
            total = gxs[r:r + 8, :] + (lower - upper)
            if not end:
                high = face(here, temp(x + 1, slice(r, r + 8)), vx[x, r:r + 8, :], vx[x + 1, r:r + 8, :])
                total = total - high
                gxs[r:r + 8, :] = high
            v = vz[x, r:r + 8, :]
            bottom = face(shift_up(here, lane), here, shift_up(v, lane), v)
            last = face(here[:, -128:], 0.0, v[:, -128:], 0.0)
            top = shift_down(bottom, lane, last)
            adv[x, r:r + 8, :] = here + 0.1 * (total + (bottom - top))

        zero = jnp.zeros((8, NZ), F32)
        temp0 = vel0 = low = low_up = zero
        for t in range(4):
            r = 8 * t
            here, v = temp(x, slice(r, r + 8)), vy[x, r:r + 8, :]
            temp1, vel1 = pltpu.roll(here, 1, 0), pltpu.roll(v, 1, 0)
            g_t = face(jnp.where(sub == 0, temp0, temp1), here, jnp.where(sub == 0, vel0, vel1), v)
            if t == 0:
                g_t = jnp.where(sub == 0, 0.0, g_t)
            g_up = pltpu.roll(g_t, 7, 0)
            if t > 0:
                finish(t - 1, low, jnp.where(sub == 7, g_up, low_up))
            temp0, vel0, low, low_up = temp1, vel1, g_t, g_up
        finish(3, low, jnp.where(sub == 7, 0.0, low_up))
        return carry

    def slabs(i, carry):
        return slab(2 * i + 1, slab(2 * i, carry))

    lax.fori_loop(0, 6, slabs, 0)
    send("t", "g")
    send("v", "g")

    lax.fori_loop(6, CUTS[0] // 2, slabs, 0)

    own_at = pl.ds(b, 1)
    inc[own_at] = snd[own_at]

    def owned(q, carry):
        src = [(j >> 1) * 8 + q * 2 + (j & 1) for j in range(PACK)]
        for i in src:
            @pl.when(i != b)
            def _():
                row_copy(i, i).wait_recv()

        field = [jnp.concatenate([inc[i][:, f * SLOTS:(f + 1) * SLOTS] for i in src], axis=1) for f in range(3)]
        code = field[2].astype(I32)
        hot = onehot(code >> 7, ROWS)
        mask = lax.broadcasted_iota(I32, (128, PACK * SLOTS), 0) == (code & 127)
        found = dot(table[...], hot)
        found = found[0:128] + found[128:256] + found[256:384]
        wall = jnp.sum(jnp.where(mask, found, 0.0), axis=0, keepdims=True)
        flux = field[1] * (field[0] - wall)
        hi = flux.astype(BF).astype(F32)
        spread = jnp.concatenate([jnp.where(mask, hi, 0.0), jnp.where(mask, flux - hi, 0.0)], axis=0)
        for j, i in enumerate(src):
            flx[i] = flux[:, j * SLOTS:(j + 1) * SLOTS]
        dep[...] += dot_nt(hot, spread.astype(BF))
        for i in src:
            @pl.when(i != b)
            def _():
                flux_copy(i, b).start()

        return carry

    lax.fori_loop(0, BLK // PACK, owned, 0)

    def sweep(k, x):
        here = cur[k, x + 1, 8:16, :]
        beside = kp[0, x] * (cur[k, x + 2, 8:16, :] + cur[k, x, 8:16, :])
        beside = beside + kp[1, x] * (cur[k, x + 1, 9:17, :] + cur[k, x + 1, 7:15, :])
        beside = beside + kp[2, x] * (shift_up(here, lane) + shift_down(here, lane, 0.0))
        return base[x] + beside

    solid_receive(0)
    for x in range(WX):
        deposit = jnp.concatenate(
            [dep[zb * 64 + x * 8:zb * 64 + x * 8 + 8, 0:128] + dep[zb * 64 + x * 8:zb * 64 + x * 8 + 8, 128:256]
             for zb in range(ZB)], axis=1)
        base[x] = (0.5 * cur[0, x + 1, 8:16, :] + deposit) * inv[x]
        cur[1, x + 1, 8:16, :] = sweep(0, x)
    solid_send(1)
    lax.fori_loop(CUTS[0] // 2, NX // 2 - 1, slabs, 0)
    slab(NX - 2, 0)
    slab(NX - 1, 0, True)
    solid_receive(1)
    for x in range(WX):
        cur[2, x + 1, 8:16, :] = sweep(1, x)
    solid_send(2)
    ret[own_at] = flx[own_at]

    def returned(k, carry):
        other = lax.rem(b + k, BLK)
        flux_copy(other, other).wait_recv()
        return carry

    lax.fori_loop(1, BLK, returned, 0)
    for j in range(BLK):
        rmat[j:j + 1, :] = ret[j]
    stacked = jnp.concatenate(list(split3(rmat[...])), axis=0).astype(BF)
    back = dot(stacked, onehot(rank_s[...], SLOTS))
    back = back[0:16] + back[16:32] + back[32:48]
    flux = jnp.sum(jnp.where(mine, back, 0.0), axis=0, keepdims=True)
    sink_weights(flux, cell_v[...], weights, rowcode)

    receive("y", "b")
    gs[...] = 0.1 * face(yrcv[0, 0], ysnd[0, 0], yrcv[0, 1], ysnd[0, 1])
    gxs[...] = 0.1 * face(ysnd[1, 0], yrcv[1, 0], ysnd[1, 1], yrcv[1, 1])

    def edge(x, carry):
        adv[x, 0:1, :] += gs[pl.ds(x, 1), :]
        adv[x, NY - 1:NY, :] -= gxs[pl.ds(x, 1), :]
        return carry

    lax.fori_loop(0, NX, edge, 0)
    receive("t", "g")
    receive("v", "g")
    adv[0] += 0.1 * face(xrcv[0, 0], temp(0, slice(0, NY)), xrcv[0, 1], vx[0])
    adv[NX - 1] -= 0.1 * face(temp(NX - 1, slice(0, NY)), xrcv[1, 0], vx[NX - 1], xrcv[1, 1])

    def sink_group(i, carry):
        total = sink(i, weights, rowcode)
        for x in range(SINK):
            for zb in range(ZB):
                at = x * 192 + zb * 32
                cols = slice(zb * 128, (zb + 1) * 128)
                adv[i * SINK + x, :, cols] += total[at:at + 32, :]
        return carry

    lax.fori_loop(0, CUTS[2], sink_group, 0)
    solid_receive(2)
    for x in range(WX):
        cur[3, x + 1, 8:16, :] = sweep(2, x)
    solid_send(3)
    lax.fori_loop(CUTS[2], NX // SINK, sink_group, 0)
    solid_receive(3)
    for x in range(WX):
        solid_out[x] = sweep(3, x)

    def drained(k, carry):
        other = lax.rem(b + k, BLK)
        row_copy(other, b).wait_send()
        flux_copy(other, b).wait_send()
        return carry

    lax.fori_loop(1, BLK, drained, 0)
    sent("t", "g")
    sent("v", "g")
    sent("y", "b")
    for k in range(4):
        sent("sx", "g", k)
        sent("sy", "b", k)


def shards(fluid, vel, solid, kond, cell, owner, target, cond):
    vmem = pl.BlockSpec(memory_space=pltpu.VMEM)
    hbm = pl.BlockSpec(memory_space=pltpu.HBM)
    dma = pltpu.SemaphoreType.DMA
    return pl.pallas_call(
        main_kernel,
        out_shape=(
            pltpu.VMEM((NX, NY, NZ), F32),
            pltpu.VMEM((WX, WY, NZ), F32),
        ),
        in_specs=[vmem] * 4 + [hbm] * 4,
        out_specs=(vmem, vmem),
        scratch_shapes=[
            pltpu.VMEM((FACES // 128, 128), I32),
            pltpu.SMEM((FACES // 128, 128), I32),
            pltpu.VMEM((ZB, NX, NY, 128), F32),
            pltpu.VMEM((NX, NY, NZ), F32),
            pltpu.VMEM((NX, NY, NZ), F32),
            pltpu.VMEM((NX, NY, NZ), F32),
            pltpu.VMEM((FACES, 128), F32),
            pltpu.VMEM((1, FACES), F32),
            pltpu.VMEM((1, FACES), I32),
            pltpu.VMEM((BLK, 1, 3 * SLOTS), F32),
            pltpu.VMEM((BLK, 1, 3 * SLOTS), F32),
            pltpu.VMEM((BLK, 1, SLOTS), F32),
            pltpu.VMEM((BLK, 1, SLOTS), F32),
            pltpu.VMEM((BLK, SLOTS), F32),
            pltpu.VMEM((2, 2, NY, NZ), F32),
            pltpu.VMEM((2, 2, NX, NZ), F32),
            pltpu.VMEM((2, 2, NX, NZ), F32),
            pltpu.VMEM((4, WX + 2, 24, NZ), F32),
            pltpu.VMEM((4, 2, WX, NZ), F32),
            pltpu.VMEM((4, 2, WX, NZ), F32),
            pltpu.VMEM((3, WX, WY, NZ), F32),
            pltpu.VMEM((WX, WY, NZ), F32),
            pltpu.VMEM((WX, WY, NZ), F32),
            pltpu.VMEM((3 * 128, ROWS), BF),
            pltpu.VMEM((ROWS, 256), F32),
            pltpu.VMEM((NX, NZ), F32),
            pltpu.VMEM((NY, NZ), F32),
            pltpu.VMEM((256, FACES), BF),
            pltpu.VMEM((1, FACES), I32),
            dma((15,)), dma((22,)), dma((22,)), dma((BLK,)), dma((BLK,)), dma((BLK,)), dma((BLK,)),
        ],
        compiler_params=pltpu.CompilerParams(
            collective_id=0, has_side_effects=True, vmem_limit_bytes=60 * 1024 * 1024),
        name="exchange",
    )(cell, owner, target, cond, fluid, vel, solid, kond)


def solution(mesh):
    in_specs = (
        P("grp", "blk", None),
        P(None, "grp", "blk", None),
        P("grp", "blk", None),
        P(None, "grp", "blk", None),
        P("grp", "blk"),
        P("grp", "blk"),
        P("grp", "blk"),
        P("grp", "blk"),
    )
    out_specs = (P("grp", "blk", None), P("grp", "blk", None))
    return jax.shard_map(shards, mesh=mesh, in_specs=in_specs, out_specs=out_specs, check_vma=False)
```

```python
import jax
import jax.numpy as jnp
from jax import lax
from jax.experimental import pallas as pl
from jax.experimental.pallas import tpu as pltpu
from jax.sharding import PartitionSpec as P

F32 = jnp.float32
BF = jnp.bfloat16
I32 = jnp.int32
MESH = pl.DeviceIdType.MESH

NX, NY, NZ = 32, 32, 768
WX, WY = 8, 8
ZB = NZ // 128
SLOTS = 512
FACES = 2048
GRP, BLK = 8, 16
LANES = 192
ROWS = WX * WY * NZ // LANES
PACK = 4
SINK = 4
CUTS = (12, 0, 4)


def split3(v):
    hi = v.astype(BF).astype(F32)
    rest = v - hi
    mid = rest.astype(BF).astype(F32)
    return hi, mid, rest - mid


def dot(a, b):
    return lax.dot_general(a, b, (((1,), (0,)), ((), ())), preferred_element_type=F32)


def dot_nt(a, b):
    return lax.dot_general(a, b, (((1,), (1,)), ((), ())), preferred_element_type=F32)


def onehot(index, count):
    rows = lax.broadcasted_iota(I32, (count, index.shape[1]), 0)
    return jnp.where(rows == index, 1.0, 0.0).astype(BF)


def face(a, b, va, vb):
    w = va + vb
    return b * w + (jnp.maximum(w, 0.0) + 0.4) * (a - b)


def shift_up(v, lane):
    r = pltpu.roll(v, 1, 1)
    first = jnp.where(lane == 0, 0.0, r[:, :128])
    return jnp.concatenate([first, r[:, 128:]], axis=1)


def shift_down(v, lane, last):
    r = pltpu.roll(v, v.shape[1] - 1, 1)
    top = jnp.where(lane == 127, last, r[:, -128:])
    return jnp.concatenate([r[:, :-128], top], axis=1)


def sink_weights(flux, cell, weights, rowcode):
    xy = ((cell >> 8) * 43691) >> 17
    zb = (cell >> 7) - 6 * xy
    rowcode[...] = (xy >> 5) * 192 + zb * 32 + (xy & 31)
    mask = lax.broadcasted_iota(I32, (128, FACES), 0) == (cell & 127)
    flux = -0.2 * flux
    hi = flux.astype(BF).astype(F32)
    weights[0:128, :] = jnp.where(mask, hi, 0.0).astype(BF)
    weights[128:256, :] = jnp.where(mask, flux - hi, 0.0).astype(BF)


def sink(group, weights, rowcode):
    hot = onehot(rowcode[...] - group * (SINK * 192), SINK * 192)
    total = dot_nt(hot, weights[...])
    return total[:, 0:128] + total[:, 128:256]


def main_kernel(
    cell_v, owner_v, target_v, cond_v, fluid, vel, solid, kond,
    adv, solid_out,
    rows_v, rows_s,
    tg, vy, vx, vz, buf, tf_s, rank_s, snd, inc, flx, ret, rmat,
    xrcv, ysnd, yrcv, cur, sysnd, syrcv, kp, inv, base, table, dep, gs, gxs, weights, rowcode,
    lsem, ssem, rsem, osem, isem, fsem, bsem,
):
    g = lax.axis_index("grp")
    b = lax.axis_index("blk")
    has = {("g", 0): g > 0, ("g", 1): g < GRP - 1, ("b", 0): b > 0, ("b", 1): b < BLK - 1}

    def neighbour(axis, side):
        step = 1 if side else -1
        return (g + step, b) if axis == "g" else (g, b + step)

    cell = cell_v[...]
    cell_xy = ((cell >> 8) * 43691) >> 17
    cell_row = ((cell >> 7) - 6 * cell_xy) * (NX * NY) + cell_xy
    for c in range(FACES // 128):
        rows_v[c:c + 1, :] = cell_row[:, c * 128:(c + 1) * 128]
    rows_copy = pltpu.make_async_copy(rows_v, rows_s, lsem.at[14])
    rows_copy.start()
    loads = []

    def load(src, dst):
        c = pltpu.make_async_copy(src, dst, lsem.at[len(loads)])
        c.start()
        loads.append(c)

    load(solid, cur.at[0, pl.ds(1, WX), pl.ds(8, WY), :])
    for zb in range(ZB):
        load(fluid.at[:, :, pl.ds(zb * 128, 128)], tg.at[zb])

    def temp(x, rows):
        return jnp.concatenate([tg[zb, x, rows, :] for zb in range(ZB)], axis=1)

    bar = pltpu.get_barrier_semaphore()

    def greet(k, carry):
        pl.semaphore_signal(bar, inc=1, device_id=(g, lax.rem(b + k, BLK)), device_id_type=MESH)
        return carry

    lax.fori_loop(1, BLK, greet, 0)
    for side in (0, 1):
        @pl.when(has["g", side])
        def _():
            pl.semaphore_signal(bar, inc=1, device_id=neighbour("g", side), device_id_type=MESH)

    for side in (0, 1):
        @pl.when(jnp.logical_not(has["g", side]))
        def _():
            xrcv[side] = jnp.zeros((2, NY, NZ), F32)
            wat = 0 if side == 0 else WX + 1
            for k in range(4):
                cur[k, wat, 8:16, :] = jnp.zeros((WY, NZ), F32)

        @pl.when(jnp.logical_not(has["b", side]))
        def _():
            yrcv[side] = jnp.zeros((2, NX, NZ), F32)
            for k in range(4):
                syrcv[k, side] = jnp.zeros((WX, NZ), F32)

    owner = owner_v[...]
    own16 = onehot(owner, BLK)
    upper = jnp.where(
        lax.broadcasted_iota(I32, (128, 128), 0) <= lax.broadcasted_iota(I32, (128, 128), 1), 1.0, 0.0
    ).astype(BF)
    inside = dot(jnp.concatenate([own16[:, c * 128:(c + 1) * 128] for c in range(FACES // 128)], axis=0), upper)
    mine = lax.broadcasted_iota(I32, (BLK, FACES), 0) == owner
    offset = jnp.full((BLK, 1), -1.0, F32)
    for c in range(FACES // 128):
        cols = slice(c * 128, (c + 1) * 128)
        running = inside[c * BLK:(c + 1) * BLK]
        rank_s[:, cols] = jnp.sum(
            jnp.where(mine[:, cols], running + offset, 0.0), axis=0, keepdims=True).astype(I32)
        offset = offset + running[:, 127:128]

    def remote(src, dst, at, device):
        return pltpu.make_async_remote_copy(
            src_ref=src, dst_ref=dst, send_sem=ssem.at[at], recv_sem=rsem.at[at],
            device_id=device, device_id_type=MESH,
        )

    def message(kind, axis, k=0):
        out = []
        for slot in (0, 1):
            side = 1 - slot
            to = neighbour(axis, side)
            if kind == "t":
                c = remote(fluid.at[NX - 1 if side else 0],
                           xrcv.at[slot, 0], slot, to)
            elif kind == "v":
                c = remote(vel.at[0, NX - 1 if side else 0], xrcv.at[slot, 1], 2 + slot, to)
            elif kind == "y":
                c = remote(ysnd.at[side], yrcv.at[slot], 4 + slot, to)
            elif kind == "sx":
                c = remote(cur.at[k, WX if side else 1, pl.ds(8, WY), :],
                           cur.at[k, WX + 1 if slot else 0, pl.ds(8, WY), :], 6 + 2 * k + slot, to)
            else:
                c = remote(sysnd.at[k, side], syrcv.at[k, slot], 14 + 2 * k + slot, to)
            out.append(c)
        return out

    def send(kind, axis, k=0):
        for slot, c in enumerate(message(kind, axis, k)):
            @pl.when(has[axis, 1 - slot])
            def _():
                c.start()

    def receive(kind, axis, k=0):
        for slot, c in enumerate(message(kind, axis, k)):
            @pl.when(has[axis, slot])
            def _():
                c.wait_recv()

    def sent(kind, axis, k=0):
        for slot, c in enumerate(message(kind, axis, k)):
            @pl.when(has[axis, 1 - slot])
            def _():
                c.wait_send()

    def solid_send(k):
        for x in range(WX):
            sysnd[k, 0, x:x + 1, :] = cur[k, x + 1, 8:9, :]
            sysnd[k, 1, x:x + 1, :] = cur[k, x + 1, 15:16, :]
        send("sx", "g", k)
        send("sy", "b", k)

    def solid_receive(k):
        receive("sx", "g", k)
        receive("sy", "b", k)
        for x in range(WX):
            cur[k, x + 1, 7:8, :] = syrcv[k, 0, x:x + 1, :]
            cur[k, x + 1, 16:17, :] = syrcv[k, 1, x:x + 1, :]

    for i in range(1, 7):
        loads[i].wait()
    load(vel.at[1], vy)
    load(vel.at[0], vx)
    load(vel.at[2], vz)
    load(kond, kp)
    rows_copy.wait()
    flat = tg.reshape(ZB * NX * NY, 128)

    def gather(i, carry):
        at = pl.multiple_of(i * 128, 128)
        for u in range(128):
            buf[pl.ds(at + u, 1), :] = flat[pl.ds(rows_s[i, u], 1), :]
        return carry

    lax.fori_loop(0, FACES // 128, gather, 0)
    lane128 = lax.broadcasted_iota(I32, (128, 128), 0)
    for c in range(FACES // 128):
        cols = slice(c * 128, (c + 1) * 128)
        block = buf[cols, :].T
        lane = cell_v[:, cols] & 127
        tf_s[:, cols] = jnp.sum(jnp.where(lane128 == lane, block, 0.0), axis=0, keepdims=True)

    target = target_v[...]
    target_xy = ((target >> 8) * 43691) >> 17
    target_z = target - NZ * target_xy
    part = ((target_z >> 6) * 43691) >> 17
    code = (part * (WX * WY) + target_xy) * LANES + (target_z - LANES * part)
    fields = list(split3(tf_s[...])) + list(split3(cond_v[...]))
    fields += [((code >> 8) << 8).astype(F32), (code & 255).astype(F32)]
    many = jnp.concatenate([jnp.where(mine, f, 0.0).astype(BF) for f in fields], axis=0)
    placed = dot_nt(many, onehot(rank_s[...], SLOTS))
    for i, (lo, hi) in enumerate(((0, 3), (3, 6), (6, 8))):
        part = placed[lo * BLK:(lo + 1) * BLK]
        for f in range(lo + 1, hi):
            part = part + placed[f * BLK:(f + 1) * BLK]
        for j in range(BLK):
            snd[j, :, i * SLOTS:(i + 1) * SLOTS] = part[j:j + 1, :]

    def row_copy(to, src):
        return pltpu.make_async_remote_copy(
            src_ref=snd.at[to], dst_ref=inc.at[b],
            send_sem=osem.at[to], recv_sem=isem.at[src], device_id=(g, to), device_id_type=MESH)

    def flux_copy(to, src):
        return pltpu.make_async_remote_copy(
            src_ref=flx.at[to], dst_ref=ret.at[b],
            send_sem=fsem.at[to], recv_sem=bsem.at[src], device_id=(g, to), device_id_type=MESH)

    def row_send(k, carry):
        row_copy(lax.rem(b + k, BLK), b).start()
        return carry

    greeted = 15 + has["g", 0].astype(I32) + has["g", 1].astype(I32)
    pl.semaphore_wait(bar, greeted)
    lax.fori_loop(1, BLK, row_send, 0)

    loads[0].wait()
    solid_send(0)
    loads[7].wait()
    lane = lax.broadcasted_iota(I32, (8, 128), 1)

    def pack(x, carry):
        for side, rows in ((0, slice(0, 1)), (1, slice(NY - 1, NY))):
            ysnd[side, 0, pl.ds(x, 1), :] = temp(x, rows)
            ysnd[side, 1, pl.ds(x, 1), :] = vy[x, rows, :]
        return carry

    lax.fori_loop(0, NX, pack, 0)
    send("y", "b")
    loads[10].wait()
    for x in range(WX):
        k0, k1, k2 = kp[0, x], kp[1, x], kp[2, x]
        r = 1.0 / (0.5 + 2.0 * (k0 + k1 + k2))
        inv[x] = r
        kp[0, x] = k0 * r
        kp[1, x] = k1 * r
        kp[2, x] = k2 * r
    block = jnp.concatenate([cur[0, x + 1, 8:16, :] for x in range(WX)], axis=0)
    quarters = [block if q == 0 else pltpu.roll(block, NZ - LANES * q, 1) for q in range(4)]
    halves = [jnp.concatenate([quarters[q][:, :256], quarters[q + 1][:, :256]], axis=0).T for q in (0, 2)]
    across = jnp.concatenate([h[:LANES] for h in halves], axis=1)
    for i, piece in enumerate(split3(across)):
        table[i * LANES:(i + 1) * LANES, :] = piece.astype(BF)
    dep[...] = jnp.zeros((2 * LANES, ROWS), F32)

    for i in range(8, 10):
        loads[i].wait()
    gxs[...] = jnp.zeros((NY, NZ), F32)
    sub = lax.broadcasted_iota(I32, (8, NZ), 0)

    def slab(x, carry, end=False):
        def finish(t, lower, upper):
            r = 8 * t
            here = temp(x, slice(r, r + 8))
            total = gxs[r:r + 8, :] + (lower - upper)
            if not end:
                high = face(here, temp(x + 1, slice(r, r + 8)), vx[x, r:r + 8, :], vx[x + 1, r:r + 8, :])
                total = total - high
                gxs[r:r + 8, :] = high
            v = vz[x, r:r + 8, :]
            bottom = face(shift_up(here, lane), here, shift_up(v, lane), v)
            last = face(here[:, -128:], 0.0, v[:, -128:], 0.0)
            top = shift_down(bottom, lane, last)
            adv[x, r:r + 8, :] = here + 0.1 * (total + (bottom - top))

        zero = jnp.zeros((8, NZ), F32)
        temp0 = vel0 = low = low_up = zero
        for t in range(4):
            r = 8 * t
            here, v = temp(x, slice(r, r + 8)), vy[x, r:r + 8, :]
            temp1, vel1 = pltpu.roll(here, 1, 0), pltpu.roll(v, 1, 0)
            g_t = face(jnp.where(sub == 0, temp0, temp1), here, jnp.where(sub == 0, vel0, vel1), v)
            if t == 0:
                g_t = jnp.where(sub == 0, 0.0, g_t)
            g_up = pltpu.roll(g_t, 7, 0)
            if t > 0:
                finish(t - 1, low, jnp.where(sub == 7, g_up, low_up))
            temp0, vel0, low, low_up = temp1, vel1, g_t, g_up
        finish(3, low, jnp.where(sub == 7, 0.0, low_up))
        return carry

    def slabs(i, carry):
        return slab(2 * i + 1, slab(2 * i, carry))

    lax.fori_loop(0, 4, slabs, 0)
    send("t", "g")
    lax.fori_loop(4, CUTS[0] // 2, slabs, 0)

    own_at = pl.ds(b, 1)
    inc[own_at] = snd[own_at]

    def owned(q, carry):
        src = [(j >> 1) * 8 + q * 2 + (j & 1) for j in range(PACK)]
        for i in src:
            @pl.when(i != b)
            def _():
                row_copy(i, i).wait_recv()

        field = [jnp.concatenate([inc[i][:, f * SLOTS:(f + 1) * SLOTS] for i in src], axis=1) for f in range(3)]
        code = field[2].astype(I32)
        row = ((code >> 6) * 43691) >> 17
        hot = onehot(row, ROWS)
        mask = lax.broadcasted_iota(I32, (LANES, PACK * SLOTS), 0) == code - LANES * row
        found = dot(table[...], hot)
        found = found[0:LANES] + found[LANES:2 * LANES] + found[2 * LANES:]
        wall = jnp.sum(jnp.where(mask, found, 0.0), axis=0, keepdims=True)
        flux = field[1] * (field[0] - wall)
        hi = flux.astype(BF).astype(F32)
        spread = jnp.concatenate([jnp.where(mask, hi, 0.0), jnp.where(mask, flux - hi, 0.0)], axis=0)
        for j, i in enumerate(src):
            flx[i] = flux[:, j * SLOTS:(j + 1) * SLOTS]
        dep[...] += dot_nt(spread.astype(BF), hot)
        for i in src:
            @pl.when(i != b)
            def _():
                flux_copy(i, b).start()

        return carry

    lax.fori_loop(0, BLK // PACK, owned, 0)

    def sweep(k, x):
        here = cur[k, x + 1, 8:16, :]
        beside = kp[0, x] * (cur[k, x + 2, 8:16, :] + cur[k, x, 8:16, :])
        beside = beside + kp[1, x] * (cur[k, x + 1, 9:17, :] + cur[k, x + 1, 7:15, :])
        beside = beside + kp[2, x] * (shift_up(here, lane) + shift_down(here, lane, 0.0))
        return base[x] + beside

    solid_receive(0)
    summed = dep[0:LANES, :] + dep[LANES:, :]
    summed = jnp.concatenate([summed, jnp.zeros((256 - LANES, ROWS), F32)], axis=0)
    deposits = jnp.zeros((WX * WY, NZ), F32)
    for h in range(2):
        half = summed[:, h * 128:(h + 1) * 128].T
        for p in range(2):
            wide = jnp.concatenate([half[p * 64:(p + 1) * 64], jnp.zeros((WX * WY, NZ - 256), F32)], axis=1)
            q = 2 * h + p
            deposits = deposits + (wide if q == 0 else pltpu.roll(wide, LANES * q, 1))
    for x in range(WX):
        deposit = deposits[x * 8:x * 8 + 8]
        base[x] = (0.5 * cur[0, x + 1, 8:16, :] + deposit) * inv[x]
        cur[1, x + 1, 8:16, :] = sweep(0, x)
    solid_send(1)
    lax.fori_loop(CUTS[0] // 2, NX // 2 - 1, slabs, 0)
    slab(NX - 2, 0)
    slab(NX - 1, 0, True)
    solid_receive(1)
    for x in range(WX):
        cur[2, x + 1, 8:16, :] = sweep(1, x)
    solid_send(2)
    ret[own_at] = flx[own_at]

    def returned(k, carry):
        other = lax.rem(b + k, BLK)
        flux_copy(other, other).wait_recv()
        return carry

    lax.fori_loop(1, BLK, returned, 0)
    send("v", "g")
    for j in range(BLK):
        rmat[j:j + 1, :] = ret[j]
    stacked = jnp.concatenate(list(split3(rmat[...])), axis=0).astype(BF)
    back = dot(stacked, onehot(rank_s[...], SLOTS))
    back = back[0:16] + back[16:32] + back[32:48]
    flux = jnp.sum(jnp.where(mine, back, 0.0), axis=0, keepdims=True)
    sink_weights(flux, cell_v[...], weights, rowcode)

    receive("y", "b")
    gs[...] = 0.1 * face(yrcv[0, 0], ysnd[0, 0], yrcv[0, 1], ysnd[0, 1])
    gxs[...] = 0.1 * face(ysnd[1, 0], yrcv[1, 0], ysnd[1, 1], yrcv[1, 1])

    def edge(x, carry):
        adv[x, 0:1, :] += gs[pl.ds(x, 1), :]
        adv[x, NY - 1:NY, :] -= gxs[pl.ds(x, 1), :]
        return carry

    lax.fori_loop(0, NX, edge, 0)
    def sink_group(i, carry):
        total = sink(i, weights, rowcode)
        for x in range(SINK):
            for zb in range(ZB):
                at = x * 192 + zb * 32
                cols = slice(zb * 128, (zb + 1) * 128)
                adv[i * SINK + x, :, cols] += total[at:at + 32, :]
        return carry

    lax.fori_loop(0, CUTS[2], sink_group, 0)
    solid_receive(2)
    for x in range(WX):
        cur[3, x + 1, 8:16, :] = sweep(2, x)
    solid_send(3)
    lax.fori_loop(CUTS[2], NX // SINK, sink_group, 0)
    receive("t", "g")
    receive("v", "g")
    adv[0] += 0.1 * face(xrcv[0, 0], temp(0, slice(0, NY)), xrcv[0, 1], vx[0])
    adv[NX - 1] -= 0.1 * face(temp(NX - 1, slice(0, NY)), xrcv[1, 0], vx[NX - 1], xrcv[1, 1])

    solid_receive(3)
    for x in range(WX):
        solid_out[x] = sweep(3, x)

    def drained(k, carry):
        other = lax.rem(b + k, BLK)
        row_copy(other, b).wait_send()
        flux_copy(other, b).wait_send()
        return carry

    lax.fori_loop(1, BLK, drained, 0)
    sent("t", "g")
    sent("v", "g")
    sent("y", "b")
    for k in range(4):
        sent("sx", "g", k)
        sent("sy", "b", k)


def shards(fluid, vel, solid, kond, cell, owner, target, cond):
    vmem = pl.BlockSpec(memory_space=pltpu.VMEM)
    hbm = pl.BlockSpec(memory_space=pltpu.HBM)
    dma = pltpu.SemaphoreType.DMA
    return pl.pallas_call(
        main_kernel,
        out_shape=(
            pltpu.VMEM((NX, NY, NZ), F32),
            pltpu.VMEM((WX, WY, NZ), F32),
        ),
        in_specs=[vmem] * 4 + [hbm] * 4,
        out_specs=(vmem, vmem),
        scratch_shapes=[
            pltpu.VMEM((FACES // 128, 128), I32),
            pltpu.SMEM((FACES // 128, 128), I32),
            pltpu.VMEM((ZB, NX, NY, 128), F32),
            pltpu.VMEM((NX, NY, NZ), F32),
            pltpu.VMEM((NX, NY, NZ), F32),
            pltpu.VMEM((NX, NY, NZ), F32),
            pltpu.VMEM((FACES, 128), F32),
            pltpu.VMEM((1, FACES), F32),
            pltpu.VMEM((1, FACES), I32),
            pltpu.VMEM((BLK, 1, 3 * SLOTS), F32),
            pltpu.VMEM((BLK, 1, 3 * SLOTS), F32),
            pltpu.VMEM((BLK, 1, SLOTS), F32),
            pltpu.VMEM((BLK, 1, SLOTS), F32),
            pltpu.VMEM((BLK, SLOTS), F32),
            pltpu.VMEM((2, 2, NY, NZ), F32),
            pltpu.VMEM((2, 2, NX, NZ), F32),
            pltpu.VMEM((2, 2, NX, NZ), F32),
            pltpu.VMEM((4, WX + 2, 24, NZ), F32),
            pltpu.VMEM((4, 2, WX, NZ), F32),
            pltpu.VMEM((4, 2, WX, NZ), F32),
            pltpu.VMEM((3, WX, WY, NZ), F32),
            pltpu.VMEM((WX, WY, NZ), F32),
            pltpu.VMEM((WX, WY, NZ), F32),
            pltpu.VMEM((3 * LANES, ROWS), BF),
            pltpu.VMEM((2 * LANES, ROWS), F32),
            pltpu.VMEM((NX, NZ), F32),
            pltpu.VMEM((NY, NZ), F32),
            pltpu.VMEM((256, FACES), BF),
            pltpu.VMEM((1, FACES), I32),
            dma((15,)), dma((22,)), dma((22,)), dma((BLK,)), dma((BLK,)), dma((BLK,)), dma((BLK,)),
        ],
        compiler_params=pltpu.CompilerParams(
            collective_id=0, has_side_effects=True, vmem_limit_bytes=60 * 1024 * 1024),
        name="exchange",
    )(cell, owner, target, cond, fluid, vel, solid, kond)


def solution(mesh):
    in_specs = (
        P("grp", "blk", None),
        P(None, "grp", "blk", None),
        P("grp", "blk", None),
        P(None, "grp", "blk", None),
        P("grp", "blk"),
        P("grp", "blk"),
        P("grp", "blk"),
        P("grp", "blk"),
    )
    out_specs = (P("grp", "blk", None), P("grp", "blk", None))
    return jax.shard_map(shards, mesh=mesh, in_specs=in_specs, out_specs=out_specs, check_vma=False)
```

```python
import jax
import jax.numpy as jnp
from jax import lax
from jax.experimental import pallas as pl
from jax.experimental.pallas import tpu as pltpu
from jax.sharding import PartitionSpec as P

F32 = jnp.float32
BF = jnp.bfloat16
I32 = jnp.int32
MESH = pl.DeviceIdType.MESH

NX, NY, NZ = 32, 32, 768
WX, WY = 8, 8
ZB = NZ // 128
SLOTS = 512
FACES = 2048
GRP, BLK = 8, 16
LANES = 192
ROWS = WX * WY * NZ // LANES
PACK = 4
SINK = 8
CUTS = (12, 2)


def split3(v):
    hi = v.astype(BF).astype(F32)
    rest = v - hi
    mid = rest.astype(BF).astype(F32)
    return hi, mid, rest - mid


def dot(a, b):
    return lax.dot_general(a, b, (((1,), (0,)), ((), ())), preferred_element_type=F32)


def dot_nt(a, b):
    return lax.dot_general(a, b, (((1,), (1,)), ((), ())), preferred_element_type=F32)


def onehot(index, count):
    rows = lax.broadcasted_iota(I32, (count, index.shape[1]), 0)
    return jnp.where(rows == index, 1.0, 0.0).astype(BF)


def face(a, b, va, vb):
    w = va + vb
    return b * w + (jnp.maximum(w, 0.0) + 0.4) * (a - b)


def shift_up(v, lane):
    r = pltpu.roll(v, 1, 1)
    first = jnp.where(lane == 0, 0.0, r[:, :128])
    return jnp.concatenate([first, r[:, 128:]], axis=1)


def shift_down(v, lane, last):
    r = pltpu.roll(v, v.shape[1] - 1, 1)
    top = jnp.where(lane == 127, last, r[:, -128:])
    return jnp.concatenate([r[:, :-128], top], axis=1)


def sink_weights(flux, cell, weights, rowcode):
    xy = ((cell >> 8) * 43691) >> 17
    zb = (cell >> 7) - 6 * xy
    rowcode[...] = (xy >> 5) * 192 + zb * 32 + (xy & 31)
    mask = lax.broadcasted_iota(I32, (128, FACES), 0) == (cell & 127)
    flux = -0.2 * flux
    hi = flux.astype(BF).astype(F32)
    weights[0:128, :] = jnp.where(mask, hi, 0.0).astype(BF)
    weights[128:256, :] = jnp.where(mask, flux - hi, 0.0).astype(BF)


def sink(group, weights, rowcode):
    hot = onehot(rowcode[...] - group * (SINK * 192), SINK * 192)
    total = dot_nt(hot, weights[...])
    return total[:, 0:128] + total[:, 128:256]


def main_kernel(
    cell_h, owner_h, target_h, cond_h, fluid, vel, solid, kond,
    adv, solid_out,
    cell_v, owner_v, target_v, cond_v, rows_v, rows_s,
    tg, vy, vx, vz, buf, tf_s, rank_s, snd, inc, flx, ret, rmat,
    xrcv, ysnd, yrcv, cur, sysnd, syrcv, kp, inv, base, table, dep, gs, gxs, weights, rowcode,
    lsem, rsmall, ssem, rsem, osem, isem, fsem, bsem,
):
    g = lax.axis_index("grp")
    b = lax.axis_index("blk")
    has = {("g", 0): g > 0, ("g", 1): g < GRP - 1, ("b", 0): b > 0, ("b", 1): b < BLK - 1}

    def neighbour(axis, side):
        step = 1 if side else -1
        return (g + step, b) if axis == "g" else (g, b + step)

    loads = []

    def load(src, dst):
        c = pltpu.make_async_copy(src, dst, lsem.at[len(loads)])
        c.start()
        loads.append(c)

    small = []
    for i, (src, dst) in enumerate(((cell_h, cell_v), (owner_h, owner_v), (target_h, target_v), (cond_h, cond_v))):
        c = pltpu.make_async_copy(src, dst, rsmall.at[i])
        c.start()
        small.append(c)
    load(solid, cur.at[0, pl.ds(1, WX), pl.ds(8, WY), :])
    for zb in range(ZB):
        load(fluid.at[:, :, pl.ds(zb * 128, 128)], tg.at[zb])

    def temp(x, rows):
        return jnp.concatenate([tg[zb, x, rows, :] for zb in range(ZB)], axis=1)

    bar = pltpu.get_barrier_semaphore()

    def greet(k, carry):
        pl.semaphore_signal(bar, inc=1, device_id=(g, lax.rem(b + k, BLK)), device_id_type=MESH)
        return carry

    lax.fori_loop(1, BLK, greet, 0)
    for side in (0, 1):
        @pl.when(has["g", side])
        def _():
            pl.semaphore_signal(bar, inc=1, device_id=neighbour("g", side), device_id_type=MESH)

    for side in (0, 1):
        @pl.when(jnp.logical_not(has["g", side]))
        def _():
            xrcv[side] = jnp.zeros((2, NY, NZ), F32)
            wat = 0 if side == 0 else WX + 1
            for k in range(4):
                cur[k, wat, 8:16, :] = jnp.zeros((WY, NZ), F32)

        @pl.when(jnp.logical_not(has["b", side]))
        def _():
            yrcv[side] = jnp.zeros((2, NX, NZ), F32)
            for k in range(4):
                syrcv[k, side] = jnp.zeros((WX, NZ), F32)

    small[0].wait()
    cell = cell_v[...]
    cell_xy = ((cell >> 8) * 43691) >> 17
    cell_row = ((cell >> 7) - 6 * cell_xy) * (NX * NY) + cell_xy
    for c in range(FACES // 128):
        rows_v[c:c + 1, :] = cell_row[:, c * 128:(c + 1) * 128]
    rows_copy = pltpu.make_async_copy(rows_v, rows_s, lsem.at[14])
    rows_copy.start()
    small[1].wait()
    owner = owner_v[...]
    own16 = onehot(owner, BLK)
    upper = jnp.where(
        lax.broadcasted_iota(I32, (128, 128), 0) <= lax.broadcasted_iota(I32, (128, 128), 1), 1.0, 0.0
    ).astype(BF)
    inside = dot(jnp.concatenate([own16[:, c * 128:(c + 1) * 128] for c in range(FACES // 128)], axis=0), upper)
    mine = lax.broadcasted_iota(I32, (BLK, FACES), 0) == owner
    offset = jnp.full((BLK, 1), -1.0, F32)
    for c in range(FACES // 128):
        cols = slice(c * 128, (c + 1) * 128)
        running = inside[c * BLK:(c + 1) * BLK]
        rank_s[:, cols] = jnp.sum(
            jnp.where(mine[:, cols], running + offset, 0.0), axis=0, keepdims=True).astype(I32)
        offset = offset + running[:, 127:128]

    def remote(src, dst, at, device):
        return pltpu.make_async_remote_copy(
            src_ref=src, dst_ref=dst, send_sem=ssem.at[at], recv_sem=rsem.at[at],
            device_id=device, device_id_type=MESH,
        )

    def message(kind, axis, k=0):
        out = []
        for slot in (0, 1):
            side = 1 - slot
            to = neighbour(axis, side)
            if kind == "t":
                c = remote(fluid.at[NX - 1 if side else 0],
                           xrcv.at[slot, 0], slot, to)
            elif kind == "v":
                c = remote(vel.at[0, NX - 1 if side else 0], xrcv.at[slot, 1], 2 + slot, to)
            elif kind == "y":
                c = remote(ysnd.at[side], yrcv.at[slot], 4 + slot, to)
            elif kind == "sx":
                c = remote(cur.at[k, WX if side else 1, pl.ds(8, WY), :],
                           cur.at[k, WX + 1 if slot else 0, pl.ds(8, WY), :], 6 + 2 * k + slot, to)
            else:
                c = remote(sysnd.at[k, side], syrcv.at[k, slot], 14 + 2 * k + slot, to)
            out.append(c)
        return out

    def send(kind, axis, k=0):
        for slot, c in enumerate(message(kind, axis, k)):
            @pl.when(has[axis, 1 - slot])
            def _():
                c.start()

    def receive(kind, axis, k=0):
        for slot, c in enumerate(message(kind, axis, k)):
            @pl.when(has[axis, slot])
            def _():
                c.wait_recv()

    def sent(kind, axis, k=0):
        for slot, c in enumerate(message(kind, axis, k)):
            @pl.when(has[axis, 1 - slot])
            def _():
                c.wait_send()

    def solid_send(k):
        for x in range(WX):
            sysnd[k, 0, x:x + 1, :] = cur[k, x + 1, 8:9, :]
            sysnd[k, 1, x:x + 1, :] = cur[k, x + 1, 15:16, :]
        send("sx", "g", k)
        send("sy", "b", k)

    def solid_receive(k):
        receive("sx", "g", k)
        receive("sy", "b", k)
        for x in range(WX):
            cur[k, x + 1, 7:8, :] = syrcv[k, 0, x:x + 1, :]
            cur[k, x + 1, 16:17, :] = syrcv[k, 1, x:x + 1, :]

    for i in range(1, 7):
        loads[i].wait()
    load(vel.at[1], vy)
    load(vel.at[0], vx)
    load(vel.at[2], vz)
    load(kond, kp)
    rows_copy.wait()
    flat = tg.reshape(ZB * NX * NY, 128)

    def gather(i, carry):
        at = pl.multiple_of(i * 128, 128)
        for u in range(128):
            buf[pl.ds(at + u, 1), :] = flat[pl.ds(rows_s[i, u], 1), :]
        return carry

    lax.fori_loop(0, FACES // 128, gather, 0)
    lane128 = lax.broadcasted_iota(I32, (128, 128), 0)
    for c in range(FACES // 128):
        cols = slice(c * 128, (c + 1) * 128)
        block = buf[cols, :].T
        lane = cell_v[:, cols] & 127
        tf_s[:, cols] = jnp.sum(jnp.where(lane128 == lane, block, 0.0), axis=0, keepdims=True)

    small[2].wait()
    small[3].wait()
    target = target_v[...]
    target_xy = ((target >> 8) * 43691) >> 17
    target_z = target - NZ * target_xy
    part = ((target_z >> 6) * 43691) >> 17
    code = (part * (WX * WY) + target_xy) * LANES + (target_z - LANES * part)
    fields = list(split3(tf_s[...])) + list(split3(cond_v[...]))
    fields += [((code >> 8) << 8).astype(F32), (code & 255).astype(F32)]
    many = jnp.concatenate([jnp.where(mine, f, 0.0).astype(BF) for f in fields], axis=0)
    placed = dot_nt(many, onehot(rank_s[...], SLOTS))
    for i, (lo, hi) in enumerate(((0, 3), (3, 6), (6, 8))):
        part = placed[lo * BLK:(lo + 1) * BLK]
        for f in range(lo + 1, hi):
            part = part + placed[f * BLK:(f + 1) * BLK]
        for j in range(BLK):
            snd[j, :, i * SLOTS:(i + 1) * SLOTS] = part[j:j + 1, :]

    def row_copy(to, src):
        return pltpu.make_async_remote_copy(
            src_ref=snd.at[to], dst_ref=inc.at[b],
            send_sem=osem.at[to], recv_sem=isem.at[src], device_id=(g, to), device_id_type=MESH)

    def flux_copy(to, src):
        return pltpu.make_async_remote_copy(
            src_ref=flx.at[to], dst_ref=ret.at[b],
            send_sem=fsem.at[to], recv_sem=bsem.at[src], device_id=(g, to), device_id_type=MESH)

    def row_send(k, carry):
        row_copy(lax.rem(b + k, BLK), b).start()
        return carry

    greeted = 15 + has["g", 0].astype(I32) + has["g", 1].astype(I32)
    pl.semaphore_wait(bar, greeted)
    lax.fori_loop(1, BLK, row_send, 0)

    loads[0].wait()
    solid_send(0)
    loads[7].wait()
    lane = lax.broadcasted_iota(I32, (8, 128), 1)

    def pack(x, carry):
        for side, rows in ((0, slice(0, 1)), (1, slice(NY - 1, NY))):
            ysnd[side, 0, pl.ds(x, 1), :] = temp(x, rows)
            ysnd[side, 1, pl.ds(x, 1), :] = vy[x, rows, :]
        return carry

    lax.fori_loop(0, NX, pack, 0)
    send("y", "b")
    for i in range(8, 10):
        loads[i].wait()
    gxs[...] = jnp.zeros((NY, NZ), F32)
    sub = lax.broadcasted_iota(I32, (8, NZ), 0)

    def slab(x, carry, end=False):
        def finish(t, lower, upper):
            r = 8 * t
            here = temp(x, slice(r, r + 8))
            total = gxs[r:r + 8, :] + (lower - upper)
            if not end:
                high = face(here, temp(x + 1, slice(r, r + 8)), vx[x, r:r + 8, :], vx[x + 1, r:r + 8, :])
                total = total - high
                gxs[r:r + 8, :] = high
            v = vz[x, r:r + 8, :]
            bottom = face(shift_up(here, lane), here, shift_up(v, lane), v)
            last = face(here[:, -128:], 0.0, v[:, -128:], 0.0)
            top = shift_down(bottom, lane, last)
            adv[x, r:r + 8, :] = here + 0.1 * (total + (bottom - top))

        zero = jnp.zeros((8, NZ), F32)
        temp0 = vel0 = low = low_up = zero
        for t in range(4):
            r = 8 * t
            here, v = temp(x, slice(r, r + 8)), vy[x, r:r + 8, :]
            temp1, vel1 = pltpu.roll(here, 1, 0), pltpu.roll(v, 1, 0)
            g_t = face(jnp.where(sub == 0, temp0, temp1), here, jnp.where(sub == 0, vel0, vel1), v)
            if t == 0:
                g_t = jnp.where(sub == 0, 0.0, g_t)
            g_up = pltpu.roll(g_t, 7, 0)
            if t > 0:
                finish(t - 1, low, jnp.where(sub == 7, g_up, low_up))
            temp0, vel0, low, low_up = temp1, vel1, g_t, g_up
        finish(3, low, jnp.where(sub == 7, 0.0, low_up))
        return carry

    def slabs(i, carry):
        return slab(2 * i + 1, slab(2 * i, carry))

    lax.fori_loop(0, 4, slabs, 0)
    send("t", "g")
    lax.fori_loop(4, CUTS[0] // 2, slabs, 0)

    loads[10].wait()
    for x in range(WX):
        k0, k1, k2 = kp[0, x], kp[1, x], kp[2, x]
        r = 1.0 / (0.5 + 2.0 * (k0 + k1 + k2))
        inv[x] = r
        kp[0, x] = k0 * r
        kp[1, x] = k1 * r
        kp[2, x] = k2 * r
    block = jnp.concatenate([cur[0, x + 1, 8:16, :] for x in range(WX)], axis=0)
    quarters = [block if q == 0 else pltpu.roll(block, NZ - LANES * q, 1) for q in range(4)]
    halves = [jnp.concatenate([quarters[q][:, :256], quarters[q + 1][:, :256]], axis=0).T for q in (0, 2)]
    across = jnp.concatenate([h[:LANES] for h in halves], axis=1)
    for i, piece in enumerate(split3(across)):
        table[i * LANES:(i + 1) * LANES, :] = piece.astype(BF)
    dep[...] = jnp.zeros((2 * LANES, ROWS), F32)

    own_at = pl.ds(b, 1)
    inc[own_at] = snd[own_at]

    def owned(q, carry):
        src = [(j >> 1) * 8 + q * 2 + (j & 1) for j in range(PACK)]
        for i in src:
            @pl.when(i != b)
            def _():
                row_copy(i, i).wait_recv()

        field = [jnp.concatenate([inc[i][:, f * SLOTS:(f + 1) * SLOTS] for i in src], axis=1) for f in range(3)]
        code = field[2].astype(I32)
        row = ((code >> 6) * 43691) >> 17
        hot = onehot(row, ROWS)
        mask = lax.broadcasted_iota(I32, (LANES, PACK * SLOTS), 0) == code - LANES * row
        found = dot(table[...], hot)
        found = found[0:LANES] + found[LANES:2 * LANES] + found[2 * LANES:]
        wall = jnp.sum(jnp.where(mask, found, 0.0), axis=0, keepdims=True)
        flux = field[1] * (field[0] - wall)
        hi = flux.astype(BF).astype(F32)
        spread = jnp.concatenate([jnp.where(mask, hi, 0.0), jnp.where(mask, flux - hi, 0.0)], axis=0)
        for j, i in enumerate(src):
            flx[i] = flux[:, j * SLOTS:(j + 1) * SLOTS]
        dep[...] += dot_nt(spread.astype(BF), hot)
        for i in src:
            @pl.when(i != b)
            def _():
                flux_copy(i, b).start()

        return carry

    lax.fori_loop(0, BLK // PACK, owned, 0)

    def sweep(k, x):
        here = cur[k, x + 1, 8:16, :]
        beside = kp[0, x] * (cur[k, x + 2, 8:16, :] + cur[k, x, 8:16, :])
        beside = beside + kp[1, x] * (cur[k, x + 1, 9:17, :] + cur[k, x + 1, 7:15, :])
        beside = beside + kp[2, x] * (shift_up(here, lane) + shift_down(here, lane, 0.0))
        return base[x] + beside

    solid_receive(0)
    summed = dep[0:LANES, :] + dep[LANES:, :]
    summed = jnp.concatenate([summed, jnp.zeros((256 - LANES, ROWS), F32)], axis=0)
    deposits = jnp.zeros((WX * WY, NZ), F32)
    for h in range(2):
        half = summed[:, h * 128:(h + 1) * 128].T
        for p in range(2):
            wide = jnp.concatenate([half[p * 64:(p + 1) * 64], jnp.zeros((WX * WY, NZ - 256), F32)], axis=1)
            q = 2 * h + p
            deposits = deposits + (wide if q == 0 else pltpu.roll(wide, LANES * q, 1))
    for x in range(WX):
        deposit = deposits[x * 8:x * 8 + 8]
        base[x] = (0.5 * cur[0, x + 1, 8:16, :] + deposit) * inv[x]
        cur[1, x + 1, 8:16, :] = sweep(0, x)
    solid_send(1)
    lax.fori_loop(CUTS[0] // 2, NX // 2 - 1, slabs, 0)
    slab(NX - 2, 0)
    slab(NX - 1, 0, True)
    solid_receive(1)
    for x in range(WX):
        cur[2, x + 1, 8:16, :] = sweep(1, x)
    solid_send(2)
    ret[own_at] = flx[own_at]

    def returned(k, carry):
        other = lax.rem(b + k, BLK)
        flux_copy(other, other).wait_recv()
        return carry

    lax.fori_loop(1, BLK, returned, 0)
    send("v", "g")
    for j in range(BLK):
        rmat[j:j + 1, :] = ret[j]
    stacked = jnp.concatenate(list(split3(rmat[...])), axis=0).astype(BF)
    back = dot(stacked, onehot(rank_s[...], SLOTS))
    back = back[0:16] + back[16:32] + back[32:48]
    flux = jnp.sum(jnp.where(mine, back, 0.0), axis=0, keepdims=True)
    sink_weights(flux, cell_v[...], weights, rowcode)

    receive("y", "b")
    gs[...] = 0.1 * face(yrcv[0, 0], ysnd[0, 0], yrcv[0, 1], ysnd[0, 1])
    gxs[...] = 0.1 * face(ysnd[1, 0], yrcv[1, 0], ysnd[1, 1], yrcv[1, 1])

    def edge(x, carry):
        adv[x, 0:1, :] += gs[pl.ds(x, 1), :]
        adv[x, NY - 1:NY, :] -= gxs[pl.ds(x, 1), :]
        return carry

    lax.fori_loop(0, NX, edge, 0)
    def sink_group(i, carry):
        total = sink(i, weights, rowcode)
        for x in range(SINK):
            for zb in range(ZB):
                at = x * 192 + zb * 32
                cols = slice(zb * 128, (zb + 1) * 128)
                adv[i * SINK + x, :, cols] += total[at:at + 32, :]
        return carry

    lax.fori_loop(0, CUTS[1], sink_group, 0)
    solid_receive(2)
    for x in range(WX):
        cur[3, x + 1, 8:16, :] = sweep(2, x)
    solid_send(3)
    lax.fori_loop(CUTS[1], NX // SINK, sink_group, 0)
    receive("t", "g")
    receive("v", "g")
    adv[0] += 0.1 * face(xrcv[0, 0], temp(0, slice(0, NY)), xrcv[0, 1], vx[0])
    adv[NX - 1] -= 0.1 * face(temp(NX - 1, slice(0, NY)), xrcv[1, 0], vx[NX - 1], xrcv[1, 1])

    solid_receive(3)
    for x in range(WX):
        solid_out[x] = sweep(3, x)

    def drained(k, carry):
        other = lax.rem(b + k, BLK)
        row_copy(other, b).wait_send()
        flux_copy(other, b).wait_send()
        return carry

    lax.fori_loop(1, BLK, drained, 0)
    sent("t", "g")
    sent("v", "g")
    sent("y", "b")
    for k in range(4):
        sent("sx", "g", k)
        sent("sy", "b", k)


def shards(fluid, vel, solid, kond, cell, owner, target, cond):
    vmem = pl.BlockSpec(memory_space=pltpu.VMEM)
    hbm = pl.BlockSpec(memory_space=pltpu.HBM)
    dma = pltpu.SemaphoreType.DMA
    return pl.pallas_call(
        main_kernel,
        out_shape=(
            pltpu.VMEM((NX, NY, NZ), F32),
            pltpu.VMEM((WX, WY, NZ), F32),
        ),
        in_specs=[hbm] * 8,
        out_specs=(vmem, vmem),
        scratch_shapes=[
            pltpu.VMEM((1, FACES), I32),
            pltpu.VMEM((1, FACES), I32),
            pltpu.VMEM((1, FACES), I32),
            pltpu.VMEM((1, FACES), F32),
            pltpu.VMEM((FACES // 128, 128), I32),
            pltpu.SMEM((FACES // 128, 128), I32),
            pltpu.VMEM((ZB, NX, NY, 128), F32),
            pltpu.VMEM((NX, NY, NZ), F32),
            pltpu.VMEM((NX, NY, NZ), F32),
            pltpu.VMEM((NX, NY, NZ), F32),
            pltpu.VMEM((FACES, 128), F32),
            pltpu.VMEM((1, FACES), F32),
            pltpu.VMEM((1, FACES), I32),
            pltpu.VMEM((BLK, 1, 3 * SLOTS), F32),
            pltpu.VMEM((BLK, 1, 3 * SLOTS), F32),
            pltpu.VMEM((BLK, 1, SLOTS), F32),
            pltpu.VMEM((BLK, 1, SLOTS), F32),
            pltpu.VMEM((BLK, SLOTS), F32),
            pltpu.VMEM((2, 2, NY, NZ), F32),
            pltpu.VMEM((2, 2, NX, NZ), F32),
            pltpu.VMEM((2, 2, NX, NZ), F32),
            pltpu.VMEM((4, WX + 2, 24, NZ), F32),
            pltpu.VMEM((4, 2, WX, NZ), F32),
            pltpu.VMEM((4, 2, WX, NZ), F32),
            pltpu.VMEM((3, WX, WY, NZ), F32),
            pltpu.VMEM((WX, WY, NZ), F32),
            pltpu.VMEM((WX, WY, NZ), F32),
            pltpu.VMEM((3 * LANES, ROWS), BF),
            pltpu.VMEM((2 * LANES, ROWS), F32),
            pltpu.VMEM((NX, NZ), F32),
            pltpu.VMEM((NY, NZ), F32),
            pltpu.VMEM((256, FACES), BF),
            pltpu.VMEM((1, FACES), I32),
            dma((15,)), dma((4,)), dma((22,)), dma((22,)), dma((BLK,)), dma((BLK,)), dma((BLK,)), dma((BLK,)),
        ],
        compiler_params=pltpu.CompilerParams(
            collective_id=0, has_side_effects=True, vmem_limit_bytes=60 * 1024 * 1024),
        name="exchange",
    )(cell, owner, target, cond, fluid, vel, solid, kond)


def solution(mesh):
    in_specs = (
        P("grp", "blk", None),
        P(None, "grp", "blk", None),
        P("grp", "blk", None),
        P(None, "grp", "blk", None),
        P("grp", "blk"),
        P("grp", "blk"),
        P("grp", "blk"),
        P("grp", "blk"),
    )
    out_specs = (P("grp", "blk", None), P("grp", "blk", None))
    return jax.shard_map(shards, mesh=mesh, in_specs=in_specs, out_specs=out_specs, check_vma=False)
```
